256 devices in a mesh: slab: 32 (over z, y), pair: 8 (over x, core).
Axes of the slice: x: 4, y: 4, z: 8, core: 2. Of those that a mesh axis runs over, the one named last changes fastest.
Arguments:
- orbitals: bfloat16 [1024, 32768], P('pair', 'slab'), may hold values from -6 to 6
- centers: int32 [1024, 3], replicated, may hold values from 0 to 16
- matchings: int32 [32, 4, 32], P('slab'), may hold values from 0 to 31, as said below
Outputs:
- exchange_force: float32 [1024, 32768], P('pair', 'slab')
The draws below stay inside these ranges and needn't reach their ends.
Inputs may be any that keep to these rules, and one draw needn't show every extreme that they name: `centers`: box corners relative to a common reference cell. `matchings`: entry [s, r, t] is the partner of member t of team s in round r; in each round every member has exactly one partner other than itself, and the partner's partner is the member.
All inputs are finite; a program needn't handle non-finite values.
Results may differ from the reference program's by a relative error of at most 0.0003.
Values may be sent and summed in bfloat16 or wider, within the bound.
A program may use at most 128 MiB of HBM per device.

```python
import math
import jax
import jax.numpy as jnp
from jax import lax

ORB_DEV = 4
BOX = 32
ROUNDS = 4
STEPS = 16
SHIFT = 8
CUT2 = 192
CELLS = 32768
TEAMS = 32
TEAM = 32
NORB = 1024
N_SLAB = 32
N_PAIR = 8


def draw_orbitals(key, part):
    key_list = jax.random.split(jax.random.fold_in(key, 29), 2)
    rough = jax.random.normal(key_list[0], (NORB, CELLS), jnp.float32)
    cell_index = jnp.arange(CELLS, dtype=jnp.int32)
    plane_coord = (cell_index // (BOX * BOX)).astype(jnp.float32)
    line_coord = (cell_index // BOX % BOX).astype(jnp.float32)
    point_coord = (cell_index % BOX).astype(jnp.float32)
    phases = jax.random.uniform(key_list[1], (NORB, 3), jnp.float32, 0.0, 2.0 * math.pi)
    angular = 2.0 * math.pi / BOX
    wave = jnp.cos(angular * plane_coord[None, :] + phases[:, 0:1])
    wave = wave + jnp.cos(angular * line_coord[None, :] + phases[:, 1:2])
    wave = (wave + jnp.cos(angular * point_coord[None, :] + phases[:, 2:3])) / 3.0
    values = 0.6 * (1.0 + 0.3 * wave) + 0.6 * rough
    return jnp.clip(values, -6.0, 6.0).astype(jnp.bfloat16)


def draw_matchings(key, part):
    key_list = jax.random.split(jax.random.fold_in(key, 17), TEAMS * ROUNDS)

    def build_matching(sub_key):
        ordering = jax.random.permutation(sub_key, TEAM).astype(jnp.int32)
        leading = ordering[0::2]
        second = ordering[1::2]
        partner = jnp.zeros((TEAM,), jnp.int32)
        partner = partner.at[leading].set(second)
        return partner.at[second].set(leading)
    return jax.vmap(build_matching)(key_list).reshape(TEAMS, ROUNDS, TEAM)


def plant(array, stream_key, low, largest):
    spot = [jax.random.randint(jax.random.fold_in(stream_key, axis), (), 0, length) for axis, length in enumerate(array.shape)]
    longest = array.shape.index(max(array.shape))
    next_to = spot[:longest] + [(spot[longest] + 1) % array.shape[longest]] + spot[longest + 1:]
    return array.at[tuple(spot)].set(low).at[tuple(next_to)].set(largest)


def setup_inputs(seed: int = 0) -> dict:
    splits = jax.random.split(jax.random.key(seed), 4)
    return {
        "orbitals": draw_orbitals(jax.random.fold_in(splits[3], 71), 0),
        "centers": plant(jax.random.randint(splits[1], (NORB, 3), 0, 2 * SHIFT + 1), jax.random.fold_in(splits[1], 1), 0, 2 * SHIFT).astype(jnp.int32),
        "matchings": draw_matchings(jax.random.fold_in(splits[3], 71), 0),
    }


SCREEN = 0.1
LOWER_BOUND = 0.1
UPPER_BOUND = 12.1


def cell_coords(box_side):
    cell_index = jnp.arange(box_side * box_side * box_side, dtype=jnp.int32)
    return cell_index // (box_side * box_side), (cell_index // box_side) % box_side, cell_index % box_side


def shift_table(offset_part, box_side):
    target = jnp.arange(box_side, dtype=jnp.int32)
    source = target[None, :, None] - offset_part.astype(jnp.int32)[:, None, None]
    return (source == target[None, None, :]).astype(jnp.float32)


def shift_rows(field, offset, box_side, shift_reach):
    row_count = field.shape[0]
    grid = field.astype(jnp.float32).reshape(row_count, box_side, box_side, box_side)
    best = lax.Precision.HIGHEST
    grid = jnp.einsum('rix,rxyz->riyz', shift_table(offset[:, 0], box_side), grid, precision=best)
    grid = jnp.einsum('riy,rxyz->rxiz', shift_table(offset[:, 1], box_side), grid, precision=best)
    grid = jnp.einsum('riz,rxyz->rxyi', shift_table(offset[:, 2], box_side), grid, precision=best)
    return grid.reshape(row_count, box_side * box_side * box_side)


def boundary_masks(box_side):
    plane_index, line_index, point_index = cell_coords(box_side)
    return jnp.stack([line_index > 0, line_index < box_side - 1, point_index > 0, point_index < box_side - 1]).astype(jnp.float32)


def apply_operator(field, box_side, masks):
    face_cells = box_side * box_side
    cell_count = field.shape[1]
    padded = jnp.pad(field, ((0, 0), (face_cells, face_cells)))

    def window(offset_cells):
        return padded[:, face_cells + offset_cells:face_cells + offset_cells + cell_count]

    neighbours = window(-face_cells) + window(face_cells)
    neighbours = neighbours + masks[0] * window(-box_side) + masks[1] * window(box_side)
    neighbours = neighbours + masks[2] * window(-1) + masks[3] * window(1)
    return (6.0 + SCREEN) * field - neighbours


def chebyshev_solve(source, box_side, sweeps):
    masks = boundary_masks(box_side)
    middle = (UPPER_BOUND + LOWER_BOUND) / 2.0
    spread = (UPPER_BOUND - LOWER_BOUND) / 2.0
    ratio = middle / spread

    def sweep(step, carry):
        solution, residual, direction, factor = carry
        solution = solution + direction
        residual = residual - apply_operator(direction, box_side, masks)
        factor_next = 1.0 / (2.0 * ratio - factor)
        direction = factor_next * factor * direction + (2.0 * factor_next / spread) * residual
        return solution, residual, direction, factor_next

    start = (jnp.zeros_like(source), source, source / middle, jnp.asarray(1.0 / ratio, source.dtype))
    return lax.fori_loop(0, sweeps, sweep, start)[0]


def pair_geometry(own_centers, partner_centers, cut_squared):
    anchor = (own_centers + partner_centers) // 2
    difference = own_centers - partner_centers
    active = (jnp.sum(difference * difference, axis=1) <= cut_squared).astype(jnp.float32)
    return own_centers - anchor, partner_centers - anchor, active


def pair_potential(own_rows, partner_rows, own_offset, partner_offset, active, box_side, shift_reach, sweeps):
    own_field = shift_rows(own_rows, own_offset, box_side, shift_reach)
    partner_field = shift_rows(partner_rows, partner_offset, box_side, shift_reach)
    density = active[:, None] * own_field * partner_field
    return chebyshev_solve(density, box_side, sweeps), own_field, partner_field


def team_forces(packed):
    team_rows, team_centers, team_matches = packed
    total = jnp.zeros(team_rows.shape, jnp.float32)
    for round_index in range(ROUNDS):
        partner = team_matches[round_index]
        own_offset, partner_offset, active = pair_geometry(team_centers, team_centers[partner], CUT2)
        potential, own_field, partner_field = pair_potential(team_rows, team_rows[partner], own_offset, partner_offset, active, BOX, SHIFT, STEPS)
        total = total + shift_rows(potential * partner_field, -own_offset, BOX, SHIFT)
    return total


def reference(orbitals, centers, matchings):
    team_rows = orbitals.reshape(N_PAIR, N_SLAB, ORB_DEV, CELLS).transpose(1, 0, 2, 3).reshape(TEAMS, TEAM, CELLS)
    team_centers = centers.reshape(N_PAIR, N_SLAB, ORB_DEV, 3).transpose(1, 0, 2, 3).reshape(TEAMS, TEAM, 3)
    forces = lax.map(team_forces, (team_rows, team_centers, matchings))
    return forces.reshape(N_SLAB, N_PAIR, ORB_DEV, CELLS).transpose(1, 0, 2, 3).reshape(NORB, CELLS)
```

```python
import functools
import jax
import jax.numpy as jnp
import numpy as np
from jax import lax
from jax.experimental import pallas as pl
from jax.experimental.pallas import tpu as pltpu
from jax.sharding import PartitionSpec as P

BOX = 32
STEPS = 16
CUT2 = 192
SCREEN = 0.1
LOWER_BOUND = 0.1
UPPER_BOUND = 12.1
ROWS = 256
LANES = 128
MARGIN = 72


def sine_table():
    index = np.arange(1, BOX + 1)
    return np.sqrt(2.0 / (BOX + 1)) * np.sin(np.pi * np.outer(index, index) / (BOX + 1))


def filter_table():
    line = 2.0 * np.cos(np.pi * np.arange(1, BOX + 1) / (BOX + 1))
    total = line[:, None, None] + line[None, :, None] + line[None, None, :]
    operator = 6.0 + SCREEN - total
    middle = (UPPER_BOUND + LOWER_BOUND) / 2.0
    spread = (UPPER_BOUND - LOWER_BOUND) / 2.0
    ratio = middle / spread
    solution = np.zeros_like(operator)
    residual = np.ones_like(operator)
    direction = residual / middle
    factor = 1.0 / ratio
    for _ in range(STEPS):
        solution = solution + direction
        residual = residual - operator * direction
        factor_next = 1.0 / (2.0 * ratio - factor)
        direction = factor_next * factor * direction + 2.0 * factor_next / spread * residual
        factor = factor_next
    return solution.reshape(BOX, BOX * BOX).astype(np.float32)


def halves(table):
    high = table.astype(jnp.bfloat16)
    low = (table - high.astype(np.float64)).astype(jnp.bfloat16)
    return high, low


def tables():
    sine = sine_table()
    plane = np.kron(sine, sine)
    plane_high, plane_low = halves(plane)

    def by_column_tile(table):
        return table.reshape(1024, 4, 256).transpose(1, 0, 2)

    line_high, line_low = halves(np.kron(np.eye(4), sine))
    line_table = np.block([[line_high, line_high], [line_low, line_low]])
    response = filter_table().reshape(BOX, 4, 256).transpose(1, 0, 2)
    return by_column_tile(plane_high), by_column_tile(plane_low), line_table, response


def split(value):
    high = value.astype(jnp.bfloat16)
    low = (value - high.astype(jnp.float32)).astype(jnp.bfloat16)
    return high, low


def dot(left, right):
    return jnp.dot(left, right, preferred_element_type=jnp.float32)


def force_kernel(
    place_ref,
    centers_ref,
    match_ref,
    boxes_ref,
    high_ref,
    low_ref,
    line_ref,
    response_ref,
    out_ref,
    padded,
    second,
    cells,
    left_high,
    left_low,
    back_high,
    back_low,
):
    team = place_ref[0]
    owner = place_ref[1]
    padded[...] = jnp.zeros_like(padded)
    lane = lax.broadcasted_iota(jnp.int32, (8, LANES), 1)
    line = 4 * lax.broadcasted_iota(jnp.int32, (8, LANES), 0) + (lane >> 5)
    point = lane & 31

    def center(member, axis):
        return centers_ref[((member >> 2) * 32 + team) * 12 + (member & 3) * 3 + axis]

    def placed(field, offset):
        flat = offset[0] * 1024 + offset[1] * 32 + offset[2]
        turn = flat & 127
        rows = flat >> 7
        padded[MARGIN : MARGIN + ROWS, :] = pltpu.roll(field, turn, axis=1)
        near = padded[pl.ds(MARGIN - rows, ROWS), :]
        far = padded[pl.ds(MARGIN - 1 - rows, ROWS), :]
        from_line = line - offset[1]
        from_point = point - offset[2]
        inside = (
            (from_line >= 0) & (from_line < BOX) & (from_point >= 0) & (from_point < BOX)
        )
        keep_near = inside & (lane >= turn)
        keep_far = inside & (lane < turn)
        near = near.reshape(BOX, 8, LANES)
        far = far.reshape(BOX, 8, LANES)
        zero = jnp.zeros_like(near)
        picked = jnp.where(keep_near[None], near, jnp.where(keep_far[None], far, zero))
        return picked.reshape(ROWS, LANES)

    def geometry(index):
        own = owner * 4 + (index & 3)
        partner = match_ref[index >> 2, own]
        own_center = [center(own, axis) for axis in range(3)]
        partner_center = [center(partner, axis) for axis in range(3)]
        anchor = [(x + y) >> 1 for x, y in zip(own_center, partner_center)]
        own_offset = [x - g for x, g in zip(own_center, anchor)]
        partner_offset = [y - g for y, g in zip(partner_center, anchor)]
        distance = sum((x - y) * (x - y) for x, y in zip(own_center, partner_center))
        active = jnp.where(distance <= CUT2, 1.0, 0.0).astype(jnp.float32)
        return own, partner, own_offset, partner_offset, active

    @pl.loop(0, 16)
    def _(index):
        own, partner, own_offset, partner_offset, active = geometry(index)
        first_field = placed(boxes_ref[own].astype(jnp.float32), own_offset)
        second_field = placed(boxes_ref[partner].astype(jnp.float32), partner_offset)
        second[index] = second_field
        cells[pl.ds(pl.multiple_of(index * ROWS, ROWS), ROWS), :] = (
            active * first_field * second_field
        )

    for tile in range(8):
        high, low = split(cells[pl.ds(tile, 512, stride=8), :])
        left_high[:, tile * LANES : (tile + 1) * LANES] = high
        left_low[:, tile * LANES : (tile + 1) * LANES] = low

    def along_plane(high, low, tile):
        total = dot(high[...], high_ref[tile])
        total = total + dot(low[...], high_ref[tile])
        return total + dot(high[...], low_ref[tile])

    def along_line(block):
        high, low = split(block)
        both = dot(line_ref[...], jnp.concatenate([high, low], axis=0))
        return both[:128] + both[128:]

    @pl.loop(0, 4)
    def _(tile):
        waves = along_plane(left_high, left_low, tile)
        response = jnp.tile(response_ref[tile], (4, 1))
        columns = pl.ds(pl.multiple_of(tile * 256, 256), 256)
        for group in range(4):
            block = along_line(waves[group * 128 : (group + 1) * 128])
            high, low = split(along_line(block * response))
            back_high[group * 128 : (group + 1) * 128, columns] = high
            back_low[group * 128 : (group + 1) * 128, columns] = low

    for tile in range(4):
        field = along_plane(back_high, back_low, tile)
        cells[pl.ds(2 * tile, 512, stride=8), :] = field[:, :LANES]
        cells[pl.ds(2 * tile + 1, 512, stride=8), :] = field[:, LANES:]

    @pl.loop(0, 16)
    def _(index):
        own, partner, own_offset, partner_offset, active = geometry(index)
        potential = cells[pl.ds(pl.multiple_of(index * ROWS, ROWS), ROWS), :]
        term = placed(potential * second[index], [-offset for offset in own_offset])
        slot = index & 3

        @pl.when(index < 4)
        def _():
            out_ref[slot] = term

        @pl.when(index >= 4)
        def _():
            out_ref[slot] = out_ref[slot] + term


def forces(place, centers, match, boxes):
    high, low, line, response = tables()
    smem = pl.BlockSpec(memory_space=pltpu.SMEM)
    vmem = pl.BlockSpec(memory_space=pltpu.VMEM)
    return pl.pallas_call(
        force_kernel,
        out_shape=jax.ShapeDtypeStruct((4, ROWS, LANES), jnp.float32),
        in_specs=[smem, smem, smem, vmem, vmem, vmem, vmem, vmem],
        out_specs=vmem,
        scratch_shapes=[
            pltpu.VMEM((ROWS + 2 * MARGIN, LANES), jnp.float32),
            pltpu.VMEM((16, ROWS, LANES), jnp.float32),
            pltpu.VMEM((16 * ROWS, LANES), jnp.float32),
            pltpu.VMEM((512, 1024), jnp.bfloat16),
            pltpu.VMEM((512, 1024), jnp.bfloat16),
            pltpu.VMEM((512, 1024), jnp.bfloat16),
            pltpu.VMEM((512, 1024), jnp.bfloat16),
        ],
        compiler_params=pltpu.CompilerParams(vmem_limit_bytes=48 * 1024 * 1024),
    )(place, centers, match, boxes, high, low, line, response)


def shards(orbitals, centers, matchings):
    slab_index = lax.axis_index("slab")
    pair_index = lax.axis_index("pair")
    pair_count = lax.axis_size("pair")
    place = jnp.stack([slab_index, pair_index]).astype(jnp.int32)
    boxes = lax.all_to_all(orbitals, "slab", split_axis=0, concat_axis=1, tiled=True)
    team = lax.all_to_all(
        jnp.broadcast_to(boxes[None], (pair_count, *boxes.shape)), "pair", 0, 0, tiled=True
    )
    team = team.reshape(32, ROWS, LANES)
    force = forces(place, centers.reshape(-1), matchings[0], team)
    force = force.reshape(4, 32, 1024)
    return lax.all_to_all(
        force.transpose(1, 0, 2), "slab", split_axis=0, concat_axis=0, tiled=True
    ).reshape(128, 1024)


def solution(mesh):
    in_specs = (P("pair", "slab"), P(), P("slab", None, None))
    out_specs = P("pair", "slab")
    return jax.shard_map(shards, mesh=mesh, in_specs=in_specs, out_specs=out_specs, check_vma=False)
```

```python
import functools
import jax
import jax.numpy as jnp
import numpy as np
from jax import lax
from jax.experimental import pallas as pl
from jax.experimental.pallas import tpu as pltpu
from jax.sharding import PartitionSpec as P

BOX = 32
STEPS = 16
CUT2 = 192
SCREEN = 0.1
LOWER_BOUND = 0.1
UPPER_BOUND = 12.1
ROWS = 256
LANES = 128
MARGIN = 72
HOPS = (0, 1, -1, 2, -2, 3, -3, 4)
MESH = pl.DeviceIdType.MESH


def sine_table():
    index = np.arange(1, BOX + 1)
    return np.sqrt(2.0 / (BOX + 1)) * np.sin(np.pi * np.outer(index, index) / (BOX + 1))


def filter_table():
    line = 2.0 * np.cos(np.pi * np.arange(1, BOX + 1) / (BOX + 1))
    total = line[:, None, None] + line[None, :, None] + line[None, None, :]
    operator = 6.0 + SCREEN - total
    middle = (UPPER_BOUND + LOWER_BOUND) / 2.0
    spread = (UPPER_BOUND - LOWER_BOUND) / 2.0
    ratio = middle / spread
    solution = np.zeros_like(operator)
    residual = np.ones_like(operator)
    direction = residual / middle
    factor = 1.0 / ratio
    for _ in range(STEPS):
        solution = solution + direction
        residual = residual - operator * direction
        factor_next = 1.0 / (2.0 * ratio - factor)
        direction = factor_next * factor * direction + 2.0 * factor_next / spread * residual
        factor = factor_next
    return solution.reshape(BOX, BOX * BOX).astype(np.float32)


def halves(table):
    high = table.astype(jnp.bfloat16)
    low = (table - high.astype(np.float64)).astype(jnp.bfloat16)
    return high, low


def tables():
    sine = sine_table()
    plane = np.kron(sine, sine)
    plane_high, plane_low = halves(plane)

    def by_column_tile(table):
        return table.reshape(1024, 4, 256).transpose(1, 0, 2)

    line_high, line_low = halves(np.kron(np.eye(4), sine))
    line_table = np.block([[line_high, line_high], [line_low, line_low]])
    response = filter_table().reshape(BOX, 4, 256).transpose(1, 0, 2)
    return by_column_tile(plane_high), by_column_tile(plane_low), line_table, response


def split(value):
    high = value.astype(jnp.bfloat16)
    low = (value - high.astype(jnp.float32)).astype(jnp.bfloat16)
    return high, low


def dot(left, right):
    return jnp.dot(left, right, preferred_element_type=jnp.float32)


def force_kernel(
    centers_ref,
    match_ref,
    boxes_ref,
    high_ref,
    low_ref,
    line_ref,
    response_ref,
    out_ref,
    force,
    send_planes,
    from_teams,
    padded,
    second,
    cells,
    left_high,
    left_low,
    back_high,
    back_low,
):
    team = lax.axis_index("slab")
    owner = lax.axis_index("pair")
    barrier = pltpu.get_barrier_semaphore()

    @pl.loop(1, 32)
    def _(step):
        pl.semaphore_signal(
            barrier, inc=1, device_id=((team + step) % 32, owner), device_id_type=MESH
        )

    padded[...] = jnp.zeros_like(padded)
    lane = lax.broadcasted_iota(jnp.int32, (8, LANES), 1)
    line = 4 * lax.broadcasted_iota(jnp.int32, (8, LANES), 0) + (lane >> 5)
    point = lane & 31

    def center(member, axis):
        return centers_ref[((member >> 2) * 32 + team) * 12 + (member & 3) * 3 + axis]

    def box(member):
        return boxes_ref[member >> 2, :, member & 3].astype(jnp.float32).reshape(ROWS, LANES)

    def placed(field, offset):
        flat = offset[0] * 1024 + offset[1] * 32 + offset[2]
        turn = flat & 127
        rows = flat >> 7
        padded[MARGIN : MARGIN + ROWS, :] = pltpu.roll(field, turn, axis=1)
        near = padded[pl.ds(MARGIN - rows, ROWS), :]
        far = padded[pl.ds(MARGIN - 1 - rows, ROWS), :]
        from_line = line - offset[1]
        from_point = point - offset[2]
        inside = (
            (from_line >= 0) & (from_line < BOX) & (from_point >= 0) & (from_point < BOX)
        )
        keep_near = inside & (lane >= turn)
        keep_far = inside & (lane < turn)
        near = near.reshape(BOX, 8, LANES)
        far = far.reshape(BOX, 8, LANES)
        zero = jnp.zeros_like(near)
        picked = jnp.where(keep_near[None], near, jnp.where(keep_far[None], far, zero))
        return picked.reshape(ROWS, LANES)

    def geometry(index):
        own = owner * 4 + (index & 3)
        partner = match_ref[index >> 2, own]
        own_center = [center(own, axis) for axis in range(3)]
        partner_center = [center(partner, axis) for axis in range(3)]
        anchor = [(x + y) >> 1 for x, y in zip(own_center, partner_center)]
        own_offset = [x - g for x, g in zip(own_center, anchor)]
        partner_offset = [y - g for y, g in zip(partner_center, anchor)]
        distance = sum((x - y) * (x - y) for x, y in zip(own_center, partner_center))
        active = jnp.where(distance <= CUT2, 1.0, 0.0).astype(jnp.float32)
        return own, partner, own_offset, partner_offset, active

    @pl.loop(0, 16)
    def _(index):
        own, partner, own_offset, partner_offset, active = geometry(index)
        first_field = placed(box(own), own_offset)
        second_field = placed(box(partner), partner_offset)
        second[index] = second_field
        cells[pl.ds(pl.multiple_of(index * ROWS, ROWS), ROWS), :] = (
            active * first_field * second_field
        )

    for tile in range(8):
        high, low = split(cells[pl.ds(tile, 512, stride=8), :])
        left_high[:, tile * LANES : (tile + 1) * LANES] = high
        left_low[:, tile * LANES : (tile + 1) * LANES] = low

    def along_plane(high, low, tile):
        total = dot(high[...], high_ref[tile])
        total = total + dot(low[...], high_ref[tile])
        return total + dot(high[...], low_ref[tile])

    def along_line(block):
        high, low = split(block)
        both = dot(line_ref[...], jnp.concatenate([high, low], axis=0))
        return both[:128] + both[128:]

    @pl.loop(0, 4)
    def _(tile):
        waves = along_plane(left_high, left_low, tile)
        response = jnp.tile(response_ref[tile], (4, 1))
        columns = pl.ds(pl.multiple_of(tile * 256, 256), 256)
        for group in range(4):
            block = along_line(waves[group * 128 : (group + 1) * 128])
            high, low = split(along_line(block * response))
            back_high[group * 128 : (group + 1) * 128, columns] = high
            back_low[group * 128 : (group + 1) * 128, columns] = low

    for tile in range(4):
        field = along_plane(back_high, back_low, tile)
        cells[pl.ds(2 * tile, 512, stride=8), :] = field[:, :LANES]
        cells[pl.ds(2 * tile + 1, 512, stride=8), :] = field[:, LANES:]

    def send(slot):
        pltpu.make_async_copy(
            force.at[slot, pl.ds(pl.multiple_of(team * 8, 8), 8)],
            out_ref.at[team, slot],
            from_teams,
        ).start()

        @pl.loop(1, 32)
        def _(step):
            target = (team + step) % 32
            pltpu.make_async_remote_copy(
                src_ref=force.at[slot, pl.ds(pl.multiple_of(target * 8, 8), 8)],
                dst_ref=out_ref.at[team, slot],
                send_sem=send_planes,
                recv_sem=from_teams,
                device_id=(target, owner),
                device_id_type=MESH,
            ).start()

    pl.semaphore_wait(barrier, 31)
    for slot in range(4):

        @pl.loop(0, 4)
        def _(turn):
            index = turn * 4 + slot
            own, partner, own_offset, partner_offset, active = geometry(index)
            potential = cells[pl.ds(pl.multiple_of(index * ROWS, ROWS), ROWS), :]
            term = placed(potential * second[index], [-offset for offset in own_offset])

            @pl.when(turn == 0)
            def _():
                force[slot] = term

            @pl.when(turn > 0)
            def _():
                force[slot] = force[slot] + term

        if slot > 0:
            send(slot - 1)
    send(3)
    pltpu.make_async_copy(out_ref, out_ref, from_teams).wait()
    sent = out_ref.at[pl.ds(0, 31)]
    pltpu.make_async_copy(sent, sent, send_planes).wait()


def gather_kernel(
    planes_ref, out_ref, send_slab, send_pair, from_slab, from_left, from_right, from_far, from_mate
):
    slab = lax.axis_index("slab")
    pair = lax.axis_index("pair")
    z = slab // 4
    y = slab % 4
    x = pair // 2
    core = pair % 2
    right = ((x + 1) % 4) * 2 + core
    left = ((x + 3) % 4) * 2 + core
    far = ((x + 2) % 4) * 2 + core
    mate = x * 2 + 1 - core

    barrier = pltpu.get_barrier_semaphore()

    @pl.loop(1, 32)
    def _(step):
        pl.semaphore_signal(
            barrier, inc=1, device_id=((slab + step) % 32, pair), device_id_type=MESH
        )

    for other in (right, left, mate):
        pl.semaphore_signal(barrier, inc=1, device_id=(slab, other), device_id_type=MESH)
    pl.semaphore_wait(barrier, 34)

    for index, hop in enumerate(HOPS):
        target_z = (z + hop + 8) % 8
        for turn in range(4):
            if hop == 0 and turn == 0:
                pltpu.make_async_copy(
                    planes_ref.at[slab], out_ref.at[pair, slab], from_slab.at[0]
                ).start()
                continue
            target = target_z * 4 + (y + turn) % 4
            pltpu.make_async_remote_copy(
                src_ref=planes_ref.at[target],
                dst_ref=out_ref.at[pair, slab],
                send_sem=send_slab,
                recv_sem=from_slab.at[index],
                device_id=(target, pair),
                device_id_type=MESH,
            ).start()

    def chunk(owner, index):
        return out_ref.at[owner, pl.ds(((z - HOPS[index] + 8) % 8) * 4, 4)]

    def transfer(owner, index, arrival, target):
        return pltpu.make_async_remote_copy(
            src_ref=chunk(owner, index),
            dst_ref=chunk(owner, index),
            send_sem=send_pair,
            recv_sem=arrival,
            device_id=(slab, target),
            device_id_type=MESH,
        )

    for step in range(8 + 2):
        if step < 8:
            transfer(pair, step, from_slab.at[step], mate).wait_recv()
            transfer(pair, step, from_left.at[step], right).start()
            transfer(pair, step, from_right.at[step], left).start()
            transfer(pair, step, from_mate, mate).start()
        index = step - 1
        if 0 <= index < 8:
            transfer(left, index, from_left.at[index], mate).wait_recv()
            if index % 2 == 0:
                transfer(left, index, from_far.at[index], right).start()
            transfer(left, index, from_mate, mate).start()
            transfer(right, index, from_right.at[index], mate).wait_recv()
            if index % 2 == 1:
                transfer(right, index, from_far.at[index], left).start()
            transfer(right, index, from_mate, mate).start()
        index = step - 2
        if 0 <= index < 8:
            transfer(far, index, from_far.at[index], mate).wait_recv()
            transfer(far, index, from_mate, mate).start()

    def drain(ref, semaphore):
        pltpu.make_async_copy(ref, ref, semaphore).wait()

    drain(out_ref.at[pl.ds(0, 4)], from_mate)
    drain(planes_ref.at[pl.ds(0, 31)], send_slab)
    drain(out_ref.at[pl.ds(0, 7)], send_pair)


def gathered(planes):
    vmem = pl.BlockSpec(memory_space=pltpu.VMEM)
    return pl.pallas_call(
        gather_kernel,
        out_shape=jax.ShapeDtypeStruct((8, 32, 4, 8, LANES), jnp.bfloat16),
        in_specs=[vmem],
        out_specs=vmem,
        scratch_shapes=[
            pltpu.SemaphoreType.DMA,
            pltpu.SemaphoreType.DMA,
            pltpu.SemaphoreType.DMA((8,)),
            pltpu.SemaphoreType.DMA((8,)),
            pltpu.SemaphoreType.DMA((8,)),
            pltpu.SemaphoreType.DMA((8,)),
            pltpu.SemaphoreType.DMA,
        ],
        compiler_params=pltpu.CompilerParams(collective_id=0, has_side_effects=True),
    )(planes)


def forces(centers, match, boxes):
    high, low, line, response = tables()
    smem = pl.BlockSpec(memory_space=pltpu.SMEM)
    vmem = pl.BlockSpec(memory_space=pltpu.VMEM)
    return pl.pallas_call(
        force_kernel,
        out_shape=jax.ShapeDtypeStruct((32, 4, 8, LANES), jnp.float32),
        in_specs=[smem, smem, vmem, vmem, vmem, vmem, vmem],
        out_specs=vmem,
        scratch_shapes=[
            pltpu.VMEM((4, ROWS, LANES), jnp.float32),
            pltpu.SemaphoreType.DMA,
            pltpu.SemaphoreType.DMA,
            pltpu.VMEM((ROWS + 2 * MARGIN, LANES), jnp.float32),
            pltpu.VMEM((16, ROWS, LANES), jnp.float32),
            pltpu.VMEM((16 * ROWS, LANES), jnp.float32),
            pltpu.VMEM((512, 1024), jnp.bfloat16),
            pltpu.VMEM((512, 1024), jnp.bfloat16),
            pltpu.VMEM((512, 1024), jnp.bfloat16),
            pltpu.VMEM((512, 1024), jnp.bfloat16),
        ],
        compiler_params=pltpu.CompilerParams(
            collective_id=1, has_side_effects=True, vmem_limit_bytes=48 * 1024 * 1024
        ),
    )(centers, match, boxes, high, low, line, response)


def shards(orbitals, centers, matchings):
    team = gathered(orbitals.reshape(32, 4, 8, LANES))
    return forces(centers.reshape(-1), matchings[0], team).reshape(128, 1024)


def solution(mesh):
    in_specs = (P("pair", "slab"), P(), P("slab", None, None))
    out_specs = P("pair", "slab")
    return jax.shard_map(shards, mesh=mesh, in_specs=in_specs, out_specs=out_specs, check_vma=False)
```

```python
import jax
import jax.numpy as jnp
import numpy as np
from jax import lax
from jax.experimental import pallas as pl
from jax.experimental.pallas import tpu as pltpu
from jax.sharding import PartitionSpec as P

BOX = 32
STEPS = 16
CUT2 = 192
SCREEN = 0.1
LOWER_BOUND = 0.1
UPPER_BOUND = 12.1
ROWS = 256
LANES = 128
MARGIN = 72
LARGEST = 32767.0
HOPS = (0, 1, -1, 2, -2, 3, -3, 4)
NEAR_LAG = 4
FAR_LAG = 8
MESH = pl.DeviceIdType.MESH


def sine_table():
    index = np.arange(1, BOX + 1)
    return np.sqrt(2.0 / (BOX + 1)) * np.sin(np.pi * np.outer(index, index) / (BOX + 1))


def filter_table():
    line = 2.0 * np.cos(np.pi * np.arange(1, BOX + 1) / (BOX + 1))
    total = line[:, None, None] + line[None, :, None] + line[None, None, :]
    operator = 6.0 + SCREEN - total
    middle = (UPPER_BOUND + LOWER_BOUND) / 2.0
    spread = (UPPER_BOUND - LOWER_BOUND) / 2.0
    ratio = middle / spread
    solution = np.zeros_like(operator)
    residual = np.ones_like(operator)
    direction = residual / middle
    factor = 1.0 / ratio
    for _ in range(STEPS):
        solution = solution + direction
        residual = residual - operator * direction
        factor_next = 1.0 / (2.0 * ratio - factor)
        direction = factor_next * factor * direction + 2.0 * factor_next / spread * residual
        factor = factor_next
    return solution


def tables():
    sine = sine_table()
    high = sine.astype(jnp.bfloat16).astype(np.float64)
    low = sine - high
    line_high = np.kron(np.eye(4), high)
    line_low = np.kron(np.eye(4), low)
    line = np.block([[line_high, line_high], [line_low, line_low]]).astype(jnp.bfloat16)
    order = np.concatenate([np.arange(0, BOX, 2), np.arange(1, BOX, 2)])
    response = filter_table()[:, order, :].reshape(BOX, 4, 256).transpose(1, 0, 2)
    half = BOX // 2
    waves_y = np.stack([sine[:half, order[:half]], sine[:half, order[half:]]])
    spread_waves = np.repeat(waves_y, BOX, axis=2)
    spread_cells = np.repeat(waves_y.transpose(0, 2, 1), BOX, axis=2)
    spread_y = np.stack([spread_waves, spread_cells])
    spread_z = np.tile(sine, (1, half))
    return (
        spread_y.astype(np.float32),
        spread_z.astype(np.float32),
        line,
        response.astype(np.float32),
    )


def split(value):
    high = value.astype(jnp.bfloat16)
    low = (value - high.astype(jnp.float32)).astype(jnp.bfloat16)
    return high, low


def dot(left, right):
    return jnp.dot(left, right, preferred_element_type=jnp.float32)


def drain(ref, semaphore):
    pltpu.make_async_copy(ref, ref, semaphore).wait()


def kernel(
    centers_ref,
    match_ref,
    orbitals_ref,
    spread_y_ref,
    spread_z_ref,
    line_ref,
    response_ref,
    out_ref,
    stage,
    planes,
    boxes,
    plane_high,
    plane_low,
    padded,
    second,
    cells,
    left_high,
    left_low,
    back_high,
    back_low,
    force,
    coded,
    scales,
    coded_in,
    scales_in,
    send_slab,
    send_pair,
    from_slab,
    from_left,
    from_right,
    from_far,
    from_mate,
    send_coded,
    send_scales,
    from_coded,
    from_scales,
):
    slab = lax.axis_index("slab")
    pair = lax.axis_index("pair")
    z = slab // 4
    y = slab % 4
    x = pair // 2
    core = pair % 2
    right = ((x + 1) % 4) * 2 + core
    left = ((x + 3) % 4) * 2 + core
    far = ((x + 2) % 4) * 2 + core
    mate = x * 2 + 1 - core

    barrier = pltpu.get_barrier_semaphore()

    @pl.loop(1, 32)
    def _(step):
        pl.semaphore_signal(
            barrier, inc=1, device_id=((slab + step) % 32, pair), device_id_type=MESH
        )

    for other in (right, left, mate):
        pl.semaphore_signal(barrier, inc=1, device_id=(slab, other), device_id_type=MESH)

    for tile in range(8):
        stage[pl.ds(tile, 128, stride=8), :] = orbitals_ref[
            :, tile * LANES : (tile + 1) * LANES
        ].astype(jnp.float32)
    planes[...] = stage[...].reshape(32, 4, 8, LANES).astype(jnp.bfloat16)
    padded[...] = jnp.zeros_like(padded)
    lane = lax.broadcasted_iota(jnp.int32, (8, LANES), 1)
    line = 4 * lax.broadcasted_iota(jnp.int32, (8, LANES), 0) + (lane >> 5)
    point = lane & 31

    for way in range(2):
        for parity in range(2):

            @pl.loop(0, 16)
            def _(row):
                product = spread_y_ref[way, parity, pl.ds(row, 1), :] * spread_z_ref[...]
                high, low = split(product)
                rows = pl.ds(pl.multiple_of(row * 32, 32), 32)
                plane_high[way, parity, rows, :] = high
                plane_low[way, parity, rows, :] = low

    pl.semaphore_wait(barrier, 34)

    for index, hop in enumerate(HOPS):
        target_z = (z + hop + 8) % 8
        for turn in range(4):
            if hop == 0 and turn == 0:
                pltpu.make_async_copy(
                    planes.at[slab], boxes.at[pair, slab], from_slab.at[0]
                ).start()
                continue
            target = target_z * 4 + (y + turn) % 4
            pltpu.make_async_remote_copy(
                src_ref=planes.at[target],
                dst_ref=boxes.at[pair, slab],
                send_sem=send_slab,
                recv_sem=from_slab.at[index],
                device_id=(target, pair),
                device_id_type=MESH,
            ).start()

    def chunk(owner, index):
        return boxes.at[owner, pl.ds(((z - HOPS[index] + 8) % 8) * 4, 4)]

    def transfer(owner, index, arrival, target):
        return pltpu.make_async_remote_copy(
            src_ref=chunk(owner, index),
            dst_ref=chunk(owner, index),
            send_sem=send_pair,
            recv_sem=arrival,
            device_id=(slab, target),
            device_id_type=MESH,
        )

    for step in range(8 + FAR_LAG):
        if step < 8:
            transfer(pair, step, from_slab.at[step], mate).wait_recv()
            transfer(pair, step, from_left.at[step], right).start()
            transfer(pair, step, from_right.at[step], left).start()
            transfer(pair, step, from_mate, mate).start()
        index = step - NEAR_LAG
        if 0 <= index < 8:
            transfer(left, index, from_left.at[index], mate).wait_recv()
            if index % 2 == 0:
                transfer(left, index, from_far.at[index], right).start()
            transfer(left, index, from_mate, mate).start()
            transfer(right, index, from_right.at[index], mate).wait_recv()
            if index % 2 == 1:
                transfer(right, index, from_far.at[index], left).start()
            transfer(right, index, from_mate, mate).start()
        index = step - FAR_LAG
        if 0 <= index < 8:
            transfer(far, index, from_far.at[index], mate).wait_recv()
            transfer(far, index, from_mate, mate).start()

    drain(boxes.at[pl.ds(0, 4)], from_mate)

    def center(member, axis):
        return centers_ref[((member >> 2) * 32 + slab) * 12 + (member & 3) * 3 + axis]

    def box(member):
        return boxes[member >> 2, :, member & 3].astype(jnp.float32).reshape(ROWS, LANES)

    def placed(field, offset):
        flat = offset[0] * 1024 + offset[1] * 32 + offset[2]
        turn = flat & 127
        rows = flat >> 7
        padded[MARGIN : MARGIN + ROWS, :] = pltpu.roll(field, turn, axis=1)
        near = padded[pl.ds(MARGIN - rows, ROWS), :]
        far = padded[pl.ds(MARGIN - 1 - rows, ROWS), :]
        from_line = line - offset[1]
        from_point = point - offset[2]
        inside = (
            (from_line >= 0) & (from_line < BOX) & (from_point >= 0) & (from_point < BOX)
        )
        keep_near = inside & (lane >= turn)
        keep_far = inside & (lane < turn)
        near = near.reshape(BOX, 8, LANES)
        far = far.reshape(BOX, 8, LANES)
        zero = jnp.zeros_like(near)
        picked = jnp.where(keep_near[None], near, jnp.where(keep_far[None], far, zero))
        return picked.reshape(ROWS, LANES)

    def geometry(index):
        own = pair * 4 + (index & 3)
        partner = match_ref[0, index >> 2, own]
        own_center = [center(own, axis) for axis in range(3)]
        partner_center = [center(partner, axis) for axis in range(3)]
        anchor = [(x + y) >> 1 for x, y in zip(own_center, partner_center)]
        own_offset = [x - g for x, g in zip(own_center, anchor)]
        partner_offset = [y - g for y, g in zip(partner_center, anchor)]
        distance = sum((x - y) * (x - y) for x, y in zip(own_center, partner_center))
        active = jnp.where(distance <= CUT2, 1.0, 0.0).astype(jnp.float32)
        return own, partner, own_offset, partner_offset, active

    @pl.loop(0, 16)
    def _(index):
        own, partner, own_offset, partner_offset, active = geometry(index)
        first_field = placed(box(own), own_offset)
        second_field = placed(box(partner), partner_offset)
        second[index] = second_field
        cells[pl.ds(pl.multiple_of(index * ROWS, ROWS), ROWS), :] = (
            active * first_field * second_field
        )

    def turned(block):
        swapped = pltpu.roll(block, 64, axis=1)
        odd = (lax.broadcasted_iota(jnp.int32, block.shape, 1) & 32) != 0
        return jnp.where(odd, pltpu.roll(swapped, 32, axis=1), pltpu.roll(swapped, 96, axis=1))

    for tile in range(4):
        lower = cells[pl.ds(tile, 512, stride=8), :]
        upper = turned(cells[pl.ds(7 - tile, 512, stride=8), :])
        columns = slice(tile * LANES, (tile + 1) * LANES)
        for parity, value in enumerate((lower + upper, lower - upper)):
            high, low = split(value)
            left_high[parity, :, columns] = high
            left_low[parity, :, columns] = low

    def along_plane(high_ref, low_ref, way, parity, columns):
        high_table = plane_high[way, parity, :, columns]
        total = dot(high_ref[parity], high_table)
        total = total + dot(low_ref[parity], high_table)
        return total + dot(high_ref[parity], plane_low[way, parity, :, columns])

    def along_line(block):
        high, low = split(block)
        both = dot(line_ref[...], jnp.concatenate([high, low], axis=0))
        return both[:128] + both[128:]

    for tile in range(4):
        parity = tile // 2
        columns = slice((tile % 2) * 256, (tile % 2 + 1) * 256)
        waves = along_plane(left_high, left_low, 0, parity, columns)
        wide = jnp.concatenate([waves[g * 128 : (g + 1) * 128] for g in range(4)], axis=1)
        response = jnp.tile(response_ref[tile], (4, 4))
        high, low = split(along_line(along_line(wide) * response))
        for group in range(4):
            rows = slice(group * 128, (group + 1) * 128)
            part = slice(group * 256, (group + 1) * 256)
            back_high[parity, rows, columns] = high[:, part]
            back_low[parity, rows, columns] = low[:, part]

    for half in range(2):
        columns = slice(half * 256, (half + 1) * 256)
        even = along_plane(back_high, back_low, 1, 0, columns)
        odd = along_plane(back_high, back_low, 1, 1, columns)
        lower = even + odd
        upper = even - odd
        for part in range(2):
            tile = half * 2 + part
            lanes = slice(part * LANES, (part + 1) * LANES)
            cells[pl.ds(tile, 512, stride=8), :] = lower[:, lanes]
            cells[pl.ds(7 - tile, 512, stride=8), :] = turned(upper[:, lanes])

    def send(half):
        slots = pl.ds(half * 2, 2)
        pltpu.make_async_copy(
            coded.at[slab, slots], coded_in.at[slab, slots], from_coded
        ).start()

        @pl.loop(1, 32)
        def _(step):
            target = (slab + step) % 32
            pltpu.make_async_remote_copy(
                src_ref=coded.at[target, slots],
                dst_ref=coded_in.at[slab, slots],
                send_sem=send_coded,
                recv_sem=from_coded,
                device_id=(target, pair),
                device_id_type=MESH,
            ).start()

    for slot in range(4):

        @pl.loop(0, 4)
        def _(turn):
            index = turn * 4 + slot
            own, partner, own_offset, partner_offset, active = geometry(index)
            potential = cells[pl.ds(pl.multiple_of(index * ROWS, ROWS), ROWS), :]
            term = placed(potential * second[index], [-offset for offset in own_offset])

            @pl.when(turn == 0)
            def _():
                force[...] = term

            @pl.when(turn > 0)
            def _():
                force[...] = force[...] + term

        field = force[...].reshape(BOX, 8, LANES)
        peak = jnp.max(jnp.max(jnp.abs(field), axis=1, keepdims=True), axis=2, keepdims=True)
        safe = jnp.maximum(peak, 1e-30)
        code = jnp.floor(field * (LARGEST / safe) + 0.5)
        coded[:, slot] = code.astype(jnp.int32).astype(jnp.int16)
        step_size = jnp.broadcast_to(safe * (1.0 / LARGEST), (BOX, 1, LANES))
        if slot == 0:
            scales[...] = step_size
        else:
            lanes = lax.broadcasted_iota(jnp.int32, (BOX, 1, LANES), 2)
            scales[...] = jnp.where(lanes >= slot, step_size, scales[...])
        if slot == 2:
            send(0)
    send(1)
    pltpu.make_async_copy(scales.at[slab], scales_in.at[slab], from_scales).start()

    @pl.loop(1, 32)
    def _(step):
        target = (slab + step) % 32
        pltpu.make_async_remote_copy(
            src_ref=scales.at[target],
            dst_ref=scales_in.at[slab],
            send_sem=send_scales,
            recv_sem=from_scales,
            device_id=(target, pair),
            device_id_type=MESH,
        ).start()

    drain(planes.at[pl.ds(0, 31)], send_slab)
    drain(boxes.at[pl.ds(0, 7)], send_pair)
    drain(scales_in, from_scales)
    drain(coded_in, from_coded)
    for slot in range(4):
        out_ref[:, slot] = (
            coded_in[:, slot].astype(jnp.int32).astype(jnp.float32)
            * scales_in[:, :, slot : slot + 1]
        )
    drain(coded.at[pl.ds(0, 31)], send_coded)
    drain(scales.at[pl.ds(0, 31)], send_scales)


def shards(orbitals, centers, matchings):
    spread_y, spread_z, line, response = tables()
    smem = pl.BlockSpec(memory_space=pltpu.SMEM)
    vmem = pl.BlockSpec(memory_space=pltpu.VMEM)
    one = pltpu.SemaphoreType.DMA
    out = pl.pallas_call(
        kernel,
        out_shape=jax.ShapeDtypeStruct((32, 4, 8, LANES), jnp.float32),
        in_specs=[smem, smem, vmem, vmem, vmem, vmem, vmem],
        out_specs=vmem,
        scratch_shapes=[
            pltpu.VMEM((1024, LANES), jnp.float32),
            pltpu.VMEM((32, 4, 8, LANES), jnp.bfloat16),
            pltpu.VMEM((8, 32, 4, 8, LANES), jnp.bfloat16),
            pltpu.VMEM((2, 2, 512, 512), jnp.bfloat16),
            pltpu.VMEM((2, 2, 512, 512), jnp.bfloat16),
            pltpu.VMEM((ROWS + 2 * MARGIN, LANES), jnp.float32),
            pltpu.VMEM((16, ROWS, LANES), jnp.float32),
            pltpu.VMEM((16 * ROWS, LANES), jnp.float32),
            pltpu.VMEM((2, 512, 512), jnp.bfloat16),
            pltpu.VMEM((2, 512, 512), jnp.bfloat16),
            pltpu.VMEM((2, 512, 512), jnp.bfloat16),
            pltpu.VMEM((2, 512, 512), jnp.bfloat16),
            pltpu.VMEM((ROWS, LANES), jnp.float32),
            pltpu.VMEM((32, 4, 8, LANES), jnp.int16),
            pltpu.VMEM((32, 1, LANES), jnp.float32),
            pltpu.VMEM((32, 4, 8, LANES), jnp.int16),
            pltpu.VMEM((32, 1, LANES), jnp.float32),
            one,
            one,
            one((8,)),
            one((8,)),
            one((8,)),
            one((8,)),
            one,
            one,
            one,
            one,
            one,
        ],
        compiler_params=pltpu.CompilerParams(
            collective_id=0, has_side_effects=True, vmem_limit_bytes=56 * 1024 * 1024
        ),
    )(centers.reshape(-1), matchings, orbitals, spread_y, spread_z, line, response)
    return out.reshape(128, 1024)


def solution(mesh):
    in_specs = (P("pair", "slab"), P(), P("slab", None, None))
    out_specs = P("pair", "slab")
    return jax.shard_map(shards, mesh=mesh, in_specs=in_specs, out_specs=out_specs, check_vma=False)
```

```python
import jax
import jax.numpy as jnp
import numpy as np
from jax import lax
from jax.experimental import pallas as pl
from jax.experimental.pallas import tpu as pltpu
from jax.sharding import PartitionSpec as P

BOX = 32
STEPS = 16
CUT2 = 192
SCREEN = 0.1
LOWER_BOUND = 0.1
UPPER_BOUND = 12.1
ROWS = 256
LANES = 128
MARGIN = 72
LARGEST = 32767.0
HOPS = (0, 1, -1, 2, -2, 3, -3, 4)
NEAR_LAG = 4
FAR_LAG = 8
MESH = pl.DeviceIdType.MESH


def sine_table():
    index = np.arange(1, BOX + 1)
    return np.sqrt(2.0 / (BOX + 1)) * np.sin(np.pi * np.outer(index, index) / (BOX + 1))


def filter_table():
    line = 2.0 * np.cos(np.pi * np.arange(1, BOX + 1) / (BOX + 1))
    total = line[:, None, None] + line[None, :, None] + line[None, None, :]
    operator = 6.0 + SCREEN - total
    middle = (UPPER_BOUND + LOWER_BOUND) / 2.0
    spread = (UPPER_BOUND - LOWER_BOUND) / 2.0
    ratio = middle / spread
    solution = np.zeros_like(operator)
    residual = np.ones_like(operator)
    direction = residual / middle
    factor = 1.0 / ratio
    for _ in range(STEPS):
        solution = solution + direction
        residual = residual - operator * direction
        factor_next = 1.0 / (2.0 * ratio - factor)
        direction = factor_next * factor * direction + 2.0 * factor_next / spread * residual
        factor = factor_next
    return solution


def tables():
    sine = sine_table()
    high = sine.astype(jnp.bfloat16).astype(np.float64)
    low = sine - high
    line_high = np.kron(np.eye(4), high)
    line_low = np.kron(np.eye(4), low)
    line = np.block([[line_high, line_high], [line_low, line_low]]).astype(jnp.bfloat16)
    order = np.concatenate([np.arange(0, BOX, 2), np.arange(1, BOX, 2)])
    response = filter_table()[:, order, :].reshape(BOX, 4, 256).transpose(1, 0, 2)
    half = BOX // 2
    waves_y = np.stack([sine[:half, order[:half]], sine[:half, order[half:]]])
    spread_waves = np.repeat(waves_y, BOX, axis=2)
    spread_cells = np.repeat(waves_y.transpose(0, 2, 1), BOX, axis=2)
    spread_y = np.stack([spread_waves, spread_cells])
    spread_z = np.tile(sine, (1, half))
    return (
        spread_y.astype(np.float32),
        spread_z.astype(np.float32),
        line,
        response.astype(np.float32),
    )


def split(value):
    high = value.astype(jnp.bfloat16)
    low = (value - high.astype(jnp.float32)).astype(jnp.bfloat16)
    return high, low


def dot(left, right):
    return jnp.dot(left, right, preferred_element_type=jnp.float32)


def drain(ref, semaphore):
    pltpu.make_async_copy(ref, ref, semaphore).wait()


def kernel(
    centers_table,
    match_table,
    orbitals_table,
    spread_y_table,
    spread_z_table,
    line_table,
    response_table,
    out_ref,
    centers_ref,
    match_ref,
    orbitals_ref,
    spread_y_ref,
    spread_z_ref,
    line_ref,
    response_ref,
    stage,
    planes,
    boxes,
    plane_high,
    plane_low,
    padded,
    first,
    second,
    cells,
    left_high,
    left_low,
    back_high,
    back_low,
    force,
    coded,
    scales,
    coded_in,
    scales_in,
    tables_done,
    send_slab,
    send_pair,
    from_slab,
    from_left,
    from_right,
    from_far,
    from_mate,
    send_coded,
    send_scales,
    from_coded,
    from_scales,
):
    slab = lax.axis_index("slab")
    pair = lax.axis_index("pair")
    z = slab // 4
    y = slab % 4
    x = pair // 2
    core = pair % 2
    right = ((x + 1) % 4) * 2 + core
    left = ((x + 3) % 4) * 2 + core
    far = ((x + 2) % 4) * 2 + core
    mate = x * 2 + 1 - core

    barrier = pltpu.get_barrier_semaphore()

    @pl.loop(1, 32)
    def _(step):
        pl.semaphore_signal(
            barrier, inc=1, device_id=((slab + step) % 32, pair), device_id_type=MESH
        )

    for other in (right, left, mate, far):
        pl.semaphore_signal(barrier, inc=1, device_id=(slab, other), device_id_type=MESH)

    copies = [
        pltpu.make_async_copy(table, ref, tables_done.at[index])
        for index, (table, ref) in enumerate(
            [
                (orbitals_table, orbitals_ref),
                (centers_table, centers_ref),
                (match_table, match_ref),
                (spread_y_table, spread_y_ref),
                (spread_z_table, spread_z_ref),
                (line_table, line_ref),
                (response_table, response_ref),
            ]
        )
    ]
    for copy in copies:
        copy.start()

    copies[0].wait()
    for tile in range(8):
        stage[pl.ds(tile, 128, stride=8), :] = orbitals_ref[
            :, tile * LANES : (tile + 1) * LANES
        ].astype(jnp.float32)
    planes[...] = stage[...].reshape(32, 4, 8, LANES).astype(jnp.bfloat16)
    padded[...] = jnp.zeros_like(padded)
    lane = lax.broadcasted_iota(jnp.int32, (8, LANES), 1)
    line = 4 * lax.broadcasted_iota(jnp.int32, (8, LANES), 0) + (lane >> 5)
    point = lane & 31

    for copy in copies[1:]:
        copy.wait()
    for way in range(2):
        for parity in range(2):

            @pl.loop(0, 16)
            def _(row):
                product = spread_y_ref[way, parity, pl.ds(row, 1), :] * spread_z_ref[...]
                high, low = split(product)
                rows = pl.ds(pl.multiple_of(row * 32, 32), 32)
                plane_high[way, parity, rows, :] = high
                plane_low[way, parity, rows, :] = low

    pl.semaphore_wait(barrier, 35)

    for index, hop in enumerate(HOPS):
        target_z = (z + hop + 8) % 8
        for turn in range(4):
            if hop == 0 and turn == 0:
                pltpu.make_async_copy(
                    planes.at[slab], boxes.at[pair, slab], from_slab.at[0]
                ).start()
                continue
            target = target_z * 4 + (y + turn) % 4
            pltpu.make_async_remote_copy(
                src_ref=planes.at[target],
                dst_ref=boxes.at[pair, slab],
                send_sem=send_slab,
                recv_sem=from_slab.at[index],
                device_id=(target, pair),
                device_id_type=MESH,
            ).start()

    def chunk(owner, index):
        return boxes.at[owner, pl.ds(((z - HOPS[index] + 8) % 8) * 4, 4)]

    def transfer(owner, index, arrival, target):
        return pltpu.make_async_remote_copy(
            src_ref=chunk(owner, index),
            dst_ref=chunk(owner, index),
            send_sem=send_pair,
            recv_sem=arrival,
            device_id=(slab, target),
            device_id_type=MESH,
        )

    def center(member, axis):
        return centers_ref[axis, ((member >> 2) * 32 + slab) * 4 + (member & 3)]

    def box(member):
        return boxes[member >> 2, :, member & 3].astype(jnp.float32).reshape(ROWS, LANES)

    def placed(field, offset):
        flat = offset[0] * 1024 + offset[1] * 32 + offset[2]
        turn = flat & 127
        rows = flat >> 7
        padded[MARGIN : MARGIN + ROWS, :] = pltpu.roll(field, turn, axis=1)
        near = padded[pl.ds(MARGIN - rows, ROWS), :]
        far = padded[pl.ds(MARGIN - 1 - rows, ROWS), :]
        from_line = line - offset[1]
        from_point = point - offset[2]
        inside = (
            (from_line >= 0) & (from_line < BOX) & (from_point >= 0) & (from_point < BOX)
        )
        keep_near = inside & (lane >= turn)
        keep_far = inside & (lane < turn)
        near = near.reshape(BOX, 8, LANES)
        far = far.reshape(BOX, 8, LANES)
        zero = jnp.zeros_like(near)
        picked = jnp.where(keep_near[None], near, jnp.where(keep_far[None], far, zero))
        return picked.reshape(ROWS, LANES)

    def geometry(index):
        own = pair * 4 + (index & 3)
        partner = match_ref[0, index >> 2, own]
        own_center = [center(own, axis) for axis in range(3)]
        partner_center = [center(partner, axis) for axis in range(3)]
        anchor = [(x + y) >> 1 for x, y in zip(own_center, partner_center)]
        own_offset = [x - g for x, g in zip(own_center, anchor)]
        partner_offset = [y - g for y, g in zip(partner_center, anchor)]
        distance = sum((x - y) * (x - y) for x, y in zip(own_center, partner_center))
        active = jnp.where(distance <= CUT2, 1.0, 0.0).astype(jnp.float32)
        return own, partner, own_offset, partner_offset, active

    for step in range(8 + FAR_LAG):
        if step < 8:
            transfer(pair, step, from_slab.at[step], mate).wait_recv()
            transfer(pair, step, from_left.at[step], right).start()
            transfer(pair, step, from_right.at[step], left).start()
            transfer(pair, step, from_far.at[step], far).start()
            transfer(pair, step, from_mate, mate).start()
        else:

            @pl.loop(2 * (step - 8), 2 * (step - 7))
            def _(index):
                own, partner, own_offset, partner_offset, active = geometry(index)
                first[index] = active * placed(box(own), own_offset)

        index = step - NEAR_LAG
        if 0 <= index < 8:
            transfer(left, index, from_left.at[index], mate).wait_recv()
            transfer(left, index, from_mate, mate).start()
            transfer(right, index, from_right.at[index], mate).wait_recv()
            transfer(right, index, from_mate, mate).start()
        index = step - FAR_LAG
        if 0 <= index < 8:
            transfer(far, index, from_far.at[index], mate).wait_recv()
            transfer(far, index, from_mate, mate).start()

    drain(boxes.at[pl.ds(0, 4)], from_mate)

    def turned(block):
        swapped = pltpu.roll(block, 64, axis=1)
        odd = (lax.broadcasted_iota(jnp.int32, block.shape, 1) & 32) != 0
        return jnp.where(odd, pltpu.roll(swapped, 32, axis=1), pltpu.roll(swapped, 96, axis=1))

    def along_plane(high_ref, low_ref, way, parity, columns):
        high_table = plane_high[way, parity, :, columns]
        total = dot(high_ref[parity], high_table)
        total = total + dot(low_ref[parity], high_table)
        return total + dot(high_ref[parity], plane_low[way, parity, :, columns])

    def along_line(block):
        high, low = split(block)
        both = dot(line_ref[...], jnp.concatenate([high, low], axis=0))
        return both[:128] + both[128:]

    def send(half):
        slots = pl.ds(half * 2, 2)
        pltpu.make_async_copy(
            coded.at[slab, slots], coded_in.at[slab, slots], from_coded
        ).start()
        pltpu.make_async_copy(
            scales.at[half * 32 + slab], scales_in.at[half * 32 + slab], from_scales
        ).start()

        @pl.loop(1, 32)
        def _(step):
            target = (slab + step) % 32
            pltpu.make_async_remote_copy(
                src_ref=coded.at[target, slots],
                dst_ref=coded_in.at[slab, slots],
                send_sem=send_coded,
                recv_sem=from_coded,
                device_id=(target, pair),
                device_id_type=MESH,
            ).start()
            pltpu.make_async_remote_copy(
                src_ref=scales.at[half * 32 + target],
                dst_ref=scales_in.at[half * 32 + slab],
                send_sem=send_scales,
                recv_sem=from_scales,
                device_id=(target, pair),
                device_id_type=MESH,
            ).start()

    for half in range(2):

        def solve_index(turn, slot):
            return turn * 4 + half * 2 + slot

        @pl.loop(0, 8)
        def _(number):
            index = solve_index(number >> 1, number & 1)
            own, partner, own_offset, partner_offset, active = geometry(index)
            second_field = placed(box(partner), partner_offset)
            second[number] = second_field
            cells[pl.ds(pl.multiple_of(number * ROWS, ROWS), ROWS), :] = (
                first[index] * second_field
            )

        for tile in range(4):
            lower = cells[pl.ds(tile, 256, stride=8), :]
            upper = turned(cells[pl.ds(7 - tile, 256, stride=8), :])
            columns = slice(tile * LANES, (tile + 1) * LANES)
            for parity, value in enumerate((lower + upper, lower - upper)):
                high, low = split(value)
                left_high[parity, :, columns] = high
                left_low[parity, :, columns] = low

        for tile in range(4):
            parity = tile // 2
            columns = slice((tile % 2) * 256, (tile % 2 + 1) * 256)
            waves = along_plane(left_high, left_low, 0, parity, columns)
            wide = jnp.concatenate([waves[:128], waves[128:]], axis=1)
            response = jnp.tile(response_ref[tile], (4, 2))
            high, low = split(along_line(along_line(wide) * response))
            for group in range(2):
                rows = slice(group * 128, (group + 1) * 128)
                part = slice(group * 256, (group + 1) * 256)
                back_high[parity, rows, columns] = high[:, part]
                back_low[parity, rows, columns] = low[:, part]

        for part in range(2):
            columns = slice(part * 256, (part + 1) * 256)
            even = along_plane(back_high, back_low, 1, 0, columns)
            odd = along_plane(back_high, back_low, 1, 1, columns)
            lower = even + odd
            upper = even - odd
            for side in range(2):
                tile = part * 2 + side
                lanes = slice(side * LANES, (side + 1) * LANES)
                cells[pl.ds(tile, 256, stride=8), :] = lower[:, lanes]
                cells[pl.ds(7 - tile, 256, stride=8), :] = turned(upper[:, lanes])

        for slot in range(2):

            @pl.loop(0, 4)
            def _(turn):
                own, partner, own_offset, partner_offset, active = geometry(
                    solve_index(turn, slot)
                )
                number = turn * 2 + slot
                potential = cells[pl.ds(pl.multiple_of(number * ROWS, ROWS), ROWS), :]
                term = placed(potential * second[number], [-offset for offset in own_offset])

                @pl.when(turn == 0)
                def _():
                    force[...] = term

                @pl.when(turn > 0)
                def _():
                    force[...] = force[...] + term

            field = force[...].reshape(BOX, 8, LANES)
            peak = jnp.max(
                jnp.max(jnp.abs(field), axis=1, keepdims=True), axis=2, keepdims=True
            )
            safe = jnp.maximum(peak, 1e-30)
            code = jnp.floor(field * (LARGEST / safe) + 0.5)
            coded[:, half * 2 + slot] = code.astype(jnp.int32).astype(jnp.int16)
            step_size = jnp.broadcast_to(safe * (1.0 / LARGEST), (BOX, 1, LANES))
            if slot == 0:
                scales[half * 32 : half * 32 + 32] = step_size
            else:
                lanes = lax.broadcasted_iota(jnp.int32, (BOX, 1, LANES), 2)
                kept = scales[half * 32 : half * 32 + 32]
                scales[half * 32 : half * 32 + 32] = jnp.where(lanes >= slot, step_size, kept)
        send(half)

    drain(planes.at[pl.ds(0, 31)], send_slab)
    drain(boxes.at[pl.ds(0, 7)], send_pair)
    drain(scales_in, from_scales)
    drain(coded_in, from_coded)
    for member in range(4):
        value = (
            coded_in[:, member].astype(jnp.int32).astype(jnp.float32)
            * scales_in[
                (member // 2) * 32 : (member // 2) * 32 + 32, :, member % 2 : member % 2 + 1
            ]
        )
        for team in range(32):
            row = (team * 4 + member) * 8
            stage[row : row + 8, :] = value[team]
    for tile in range(8):
        out_ref[:, tile * LANES : (tile + 1) * LANES] = stage[pl.ds(tile, 128, stride=8), :]
    drain(coded.at[pl.ds(0, 31)], send_coded)
    drain(scales.at[pl.ds(0, 62)], send_scales)


def shards(orbitals, centers, matchings):
    spread_y, spread_z, line, response = tables()
    vmem = pl.BlockSpec(memory_space=pltpu.VMEM)
    one = pltpu.SemaphoreType.DMA
    hbm = pl.BlockSpec(memory_space=pltpu.HBM)
    return pl.pallas_call(
        kernel,
        out_shape=jax.ShapeDtypeStruct((128, 1024), jnp.float32),
        in_specs=[hbm] * 7,
        out_specs=vmem,
        scratch_shapes=[
            pltpu.SMEM((3, 1024), jnp.int32),
            pltpu.SMEM((1, 4, 32), jnp.int32),
            pltpu.VMEM((128, 1024), jnp.bfloat16),
            pltpu.VMEM(spread_y.shape, jnp.float32),
            pltpu.VMEM(spread_z.shape, jnp.float32),
            pltpu.VMEM(line.shape, jnp.bfloat16),
            pltpu.VMEM(response.shape, jnp.float32),
            pltpu.VMEM((1024, LANES), jnp.float32),
            pltpu.VMEM((32, 4, 8, LANES), jnp.bfloat16),
            pltpu.VMEM((8, 32, 4, 8, LANES), jnp.bfloat16),
            pltpu.VMEM((2, 2, 512, 512), jnp.bfloat16),
            pltpu.VMEM((2, 2, 512, 512), jnp.bfloat16),
            pltpu.VMEM((ROWS + 2 * MARGIN, LANES), jnp.float32),
            pltpu.VMEM((16, ROWS, LANES), jnp.float32),
            pltpu.VMEM((8, ROWS, LANES), jnp.float32),
            pltpu.VMEM((8 * ROWS, LANES), jnp.float32),
            pltpu.VMEM((2, 256, 512), jnp.bfloat16),
            pltpu.VMEM((2, 256, 512), jnp.bfloat16),
            pltpu.VMEM((2, 256, 512), jnp.bfloat16),
            pltpu.VMEM((2, 256, 512), jnp.bfloat16),
            pltpu.VMEM((ROWS, LANES), jnp.float32),
            pltpu.VMEM((32, 4, 8, LANES), jnp.int16),
            pltpu.VMEM((64, 1, LANES), jnp.float32),
            pltpu.VMEM((32, 4, 8, LANES), jnp.int16),
            pltpu.VMEM((64, 1, LANES), jnp.float32),
            one((7,)),
            one,
            one,
            one((8,)),
            one((8,)),
            one((8,)),
            one((8,)),
            one,
            one,
            one,
            one,
            one,
        ],
        compiler_params=pltpu.CompilerParams(
            collective_id=0, has_side_effects=True, vmem_limit_bytes=63 * 1024 * 1024
        ),
    )(centers.T, matchings, orbitals, spread_y, spread_z, line, response)


def solution(mesh):
    in_specs = (P("pair", "slab"), P(), P("slab", None, None))
    out_specs = P("pair", "slab")
    return jax.shard_map(shards, mesh=mesh, in_specs=in_specs, out_specs=out_specs, check_vma=False)
```

```python
import jax
import jax.numpy as jnp
import numpy as np
from jax import lax
from jax.experimental import pallas as pl
from jax.experimental.pallas import tpu as pltpu
from jax.sharding import PartitionSpec as P

BOX = 32
STEPS = 16
CUT2 = 192
SCREEN = 0.1
LOWER_BOUND = 0.1
UPPER_BOUND = 12.1
ROWS = 256
LANES = 128
MARGIN = 72
LARGEST = 32767.0
HOPS = (0, 1, -1, 2, -2, 3, -3, 4)
NEAR_LAG = 4
FAR_LAG = 8
RELAYED = 4
WAYS = 4
MESH = pl.DeviceIdType.MESH


def sine_table():
    index = np.arange(1, BOX + 1)
    return np.sqrt(2.0 / (BOX + 1)) * np.sin(np.pi * np.outer(index, index) / (BOX + 1))


def filter_table():
    line = 2.0 * np.cos(np.pi * np.arange(1, BOX + 1) / (BOX + 1))
    total = line[:, None, None] + line[None, :, None] + line[None, None, :]
    operator = 6.0 + SCREEN - total
    middle = (UPPER_BOUND + LOWER_BOUND) / 2.0
    spread = (UPPER_BOUND - LOWER_BOUND) / 2.0
    ratio = middle / spread
    solution = np.zeros_like(operator)
    residual = np.ones_like(operator)
    direction = residual / middle
    factor = 1.0 / ratio
    for _ in range(STEPS):
        solution = solution + direction
        residual = residual - operator * direction
        factor_next = 1.0 / (2.0 * ratio - factor)
        direction = factor_next * factor * direction + 2.0 * factor_next / spread * residual
        factor = factor_next
    return solution


def tables():
    sine = sine_table()
    high = sine.astype(jnp.bfloat16).astype(np.float64)
    low = sine - high
    line_high = np.kron(np.eye(4), high)
    line_low = np.kron(np.eye(4), low)
    line = np.block([[line_high, line_high], [line_low, line_low]]).astype(jnp.bfloat16)
    order = np.concatenate([np.arange(0, BOX, 2), np.arange(1, BOX, 2)])
    response = filter_table()[:, order, :].reshape(BOX, 4, 1, 256)
    response = np.tile(response, (1, 1, 2, 1)).reshape(BOX, 2048)
    half = BOX // 2
    waves_y = np.stack([sine[:half, order[:half]], sine[:half, order[half:]]])
    spread_waves = np.repeat(waves_y, BOX, axis=2)
    spread_cells = np.repeat(waves_y.transpose(0, 2, 1), BOX, axis=2)
    spread_y = np.stack([spread_waves, spread_cells])
    spread_z = np.tile(sine, (1, half))
    return (
        spread_y.astype(np.float32),
        spread_z.astype(np.float32),
        line,
        response.astype(np.float32),
    )


def split(value):
    high = value.astype(jnp.bfloat16)
    low = (value - high.astype(jnp.float32)).astype(jnp.bfloat16)
    return high, low


def dot(left, right):
    return jnp.dot(left, right, preferred_element_type=jnp.float32)


def drain(ref, semaphore):
    pltpu.make_async_copy(ref, ref, semaphore).wait()


def kernel(
    centers_table,
    match_table,
    orbitals_table,
    spread_y_table,
    spread_z_table,
    line_table,
    response_table,
    out_ref,
    centers_ref,
    match_ref,
    orbitals_ref,
    spread_y_ref,
    spread_z_ref,
    line_ref,
    response_ref,
    stage,
    planes,
    boxes,
    plane_high,
    plane_low,
    padded,
    first,
    second,
    cells,
    left_high,
    left_low,
    back_high,
    back_low,
    lines,
    lines_back,
    force,
    coded,
    scales,
    coded_in,
    scales_in,
    tables_done,
    send_slab,
    send_pair,
    from_slab,
    from_left,
    from_right,
    from_far,
    from_mate,
    send_coded,
    send_scales,
    from_coded,
    from_scales,
):
    slab = lax.axis_index("slab")
    pair = lax.axis_index("pair")
    z = slab // 4
    y = slab % 4
    x = pair // 2
    core = pair % 2
    right = ((x + 1) % 4) * 2 + core
    left = ((x + 3) % 4) * 2 + core
    far = ((x + 2) % 4) * 2 + core
    mate = x * 2 + 1 - core

    barrier = pltpu.get_barrier_semaphore()

    @pl.loop(1, 32)
    def _(step):
        pl.semaphore_signal(
            barrier, inc=1, device_id=((slab + step) % 32, pair), device_id_type=MESH
        )

    for other in (right, left, mate, far):
        pl.semaphore_signal(barrier, inc=1, device_id=(slab, other), device_id_type=MESH)

    copies = [
        pltpu.make_async_copy(table, ref, tables_done.at[index])
        for index, (table, ref) in enumerate(
            [
                (orbitals_table, orbitals_ref),
                (centers_table, centers_ref),
                (match_table, match_ref),
                (spread_y_table, spread_y_ref),
                (spread_z_table, spread_z_ref),
                (line_table, line_ref),
                (response_table, response_ref),
            ]
        )
    ]
    for copy in copies:
        copy.start()

    copies[0].wait()
    for tile in range(8):
        stage[pl.ds(tile, 128, stride=8), :] = orbitals_ref[
            :, tile * LANES : (tile + 1) * LANES
        ].astype(jnp.float32)
    planes[...] = stage[...].reshape(32, 4, 8, LANES).astype(jnp.bfloat16)
    padded[...] = jnp.zeros_like(padded)
    lane = lax.broadcasted_iota(jnp.int32, (8, LANES), 1)
    line = 4 * lax.broadcasted_iota(jnp.int32, (8, LANES), 0) + (lane >> 5)
    point = lane & 31

    for copy in copies[1:]:
        copy.wait()
    for way in range(2):
        for parity in range(2):

            @pl.loop(0, 16)
            def _(row):
                product = spread_y_ref[way, parity, pl.ds(row, 1), :] * spread_z_ref[...]
                high, low = split(product)
                rows = pl.ds(pl.multiple_of(row * 32, 32), 32)
                plane_high[way, parity, rows, :] = high
                plane_low[way, parity, rows, :] = low

    pl.semaphore_wait(barrier, 35)

    for index, hop in enumerate(HOPS):
        target_z = (z + hop + 8) % 8
        for turn in range(4):
            if hop == 0 and turn == 0:
                pltpu.make_async_copy(
                    planes.at[slab], boxes.at[pair, slab], from_slab.at[0]
                ).start()
                continue
            target = target_z * 4 + (y + turn) % 4
            pltpu.make_async_remote_copy(
                src_ref=planes.at[target],
                dst_ref=boxes.at[pair, slab],
                send_sem=send_slab,
                recv_sem=from_slab.at[index],
                device_id=(target, pair),
                device_id_type=MESH,
            ).start()

    def chunk(owner, index):
        return boxes.at[owner, pl.ds(((z - HOPS[index] + 8) % 8) * 4, 4)]

    def transfer(owner, index, arrival, target):
        return pltpu.make_async_remote_copy(
            src_ref=chunk(owner, index),
            dst_ref=chunk(owner, index),
            send_sem=send_pair,
            recv_sem=arrival,
            device_id=(slab, target),
            device_id_type=MESH,
        )

    def center(member, axis):
        return centers_ref[axis, ((member >> 2) * 32 + slab) * 4 + (member & 3)]

    def box(member):
        return boxes[member >> 2, :, member & 3].astype(jnp.float32).reshape(ROWS, LANES)

    def placed(field, offset, way):
        flat = offset[0] * 1024 + offset[1] * 32 + offset[2]
        turn = flat & 127
        rows = flat >> 7
        padded[way, MARGIN : MARGIN + ROWS, :] = pltpu.roll(field, turn, axis=1)
        near = padded[way, pl.ds(MARGIN - rows, ROWS), :]
        far = padded[way, pl.ds(MARGIN - 1 - rows, ROWS), :]
        from_line = line - offset[1]
        from_point = point - offset[2]
        inside = (
            (from_line >= 0) & (from_line < BOX) & (from_point >= 0) & (from_point < BOX)
        )
        keep_near = inside & (lane >= turn)
        keep_far = inside & (lane < turn)
        near = near.reshape(BOX, 8, LANES)
        far = far.reshape(BOX, 8, LANES)
        zero = jnp.zeros_like(near)
        picked = jnp.where(keep_near[None], near, jnp.where(keep_far[None], far, zero))
        return picked.reshape(ROWS, LANES)

    def geometry(index):
        own = pair * 4 + (index & 3)
        partner = match_ref[0, index >> 2, own]
        own_center = [center(own, axis) for axis in range(3)]
        partner_center = [center(partner, axis) for axis in range(3)]
        anchor = [(x + y) >> 1 for x, y in zip(own_center, partner_center)]
        own_offset = [x - g for x, g in zip(own_center, anchor)]
        partner_offset = [y - g for y, g in zip(partner_center, anchor)]
        distance = sum((x - y) * (x - y) for x, y in zip(own_center, partner_center))
        active = jnp.where(distance <= CUT2, 1.0, 0.0).astype(jnp.float32)
        return own, partner, own_offset, partner_offset, active

    for step in range(8 + FAR_LAG):
        if step < 8:
            transfer(pair, step, from_slab.at[step], mate).wait_recv()
            transfer(pair, step, from_left.at[step], right).start()
            transfer(pair, step, from_right.at[step], left).start()
            if step >= RELAYED:
                transfer(pair, step, from_far.at[step], far).start()
            transfer(pair, step, from_mate, mate).start()
        else:

            @pl.loop(2 * (step - 8), 2 * (step - 7))
            def _(index):
                own, partner, own_offset, partner_offset, active = geometry(index)
                first[index] = active * placed(box(own), own_offset, 0)

        index = step - NEAR_LAG
        if 0 <= index < 8:
            transfer(left, index, from_left.at[index], mate).wait_recv()
            if index < RELAYED and index % 2 == 0:
                transfer(left, index, from_far.at[index], right).start()
            transfer(left, index, from_mate, mate).start()
            transfer(right, index, from_right.at[index], mate).wait_recv()
            if index < RELAYED and index % 2 == 1:
                transfer(right, index, from_far.at[index], left).start()
            transfer(right, index, from_mate, mate).start()
        index = step - FAR_LAG
        if 0 <= index < 8:
            transfer(far, index, from_far.at[index], mate).wait_recv()
            transfer(far, index, from_mate, mate).start()

    drain(boxes.at[pl.ds(0, 4)], from_mate)

    def turned(block):
        swapped = pltpu.roll(block, 64, axis=1)
        odd = (lax.broadcasted_iota(jnp.int32, block.shape, 1) & 32) != 0
        return jnp.where(odd, pltpu.roll(swapped, 32, axis=1), pltpu.roll(swapped, 96, axis=1))

    def along_plane(high_ref, low_ref, way, parity, columns):
        high_table = plane_high[way, parity, :, columns]
        total = dot(high_ref[parity], high_table)
        total = total + dot(low_ref[parity], high_table)
        return total + dot(high_ref[parity], plane_low[way, parity, :, columns])

    def send(half):
        slots = pl.ds(half * 2, 2)
        pltpu.make_async_copy(
            coded.at[slab, slots], coded_in.at[slab, slots], from_coded
        ).start()
        pltpu.make_async_copy(
            scales.at[half * 32 + slab], scales_in.at[half * 32 + slab], from_scales
        ).start()

        @pl.loop(1, 32)
        def _(step):
            target = (slab + step) % 32
            pltpu.make_async_remote_copy(
                src_ref=coded.at[target, slots],
                dst_ref=coded_in.at[slab, slots],
                send_sem=send_coded,
                recv_sem=from_coded,
                device_id=(target, pair),
                device_id_type=MESH,
            ).start()
            pltpu.make_async_remote_copy(
                src_ref=scales.at[half * 32 + target],
                dst_ref=scales_in.at[half * 32 + slab],
                send_sem=send_scales,
                recv_sem=from_scales,
                device_id=(target, pair),
                device_id_type=MESH,
            ).start()

    for half in range(2):

        def solve_index(turn, slot):
            return turn * 4 + half * 2 + slot

        @pl.loop(0, 8 // WAYS)
        def _(step):
            for way in range(WAYS):
                number = step * WAYS + way
                index = solve_index(number >> 1, number & 1)
                own, partner, own_offset, partner_offset, active = geometry(index)
                second_field = placed(box(partner), partner_offset, way)
                second[number] = second_field
                cells[pl.ds(pl.multiple_of(number * ROWS, ROWS), ROWS), :] = (
                    first[index] * second_field
                )

        for tile in range(4):
            lower = cells[pl.ds(tile, 256, stride=8), :]
            upper = turned(cells[pl.ds(7 - tile, 256, stride=8), :])
            columns = slice(tile * LANES, (tile + 1) * LANES)
            for parity, value in enumerate((lower + upper, lower - upper)):
                high, low = split(value)
                left_high[parity, :, columns] = high
                left_low[parity, :, columns] = low

        for tile in range(4):
            parity = tile // 2
            columns = slice((tile % 2) * 256, (tile % 2 + 1) * 256)
            high, low = split(along_plane(left_high, left_low, 0, parity, columns))
            for group in range(2):
                rows = slice(group * 128, (group + 1) * 128)
                part = slice((tile * 2 + group) * 256, (tile * 2 + group + 1) * 256)
                lines[:128, part] = high[rows]
                lines[128:, part] = low[rows]

        for start in range(0, 2048, 512):
            columns = slice(start, start + 512)
            both = dot(line_ref[...], lines[:, columns])
            response = jnp.tile(response_ref[:, columns], (4, 1))
            high, low = split((both[:128] + both[128:]) * response)
            lines_back[:128, columns] = high
            lines_back[128:, columns] = low

        for start in range(0, 2048, 512):
            columns = slice(start, start + 512)
            both = dot(line_ref[...], lines_back[:, columns])
            high, low = split(both[:128] + both[128:])
            for block in range(2):
                place = start // 256 + block
                tile = place // 2
                group = place % 2
                rows = slice(group * 128, (group + 1) * 128)
                part = slice(block * 256, (block + 1) * 256)
                columns = slice((tile % 2) * 256, (tile % 2 + 1) * 256)
                back_high[tile // 2, rows, columns] = high[:, part]
                back_low[tile // 2, rows, columns] = low[:, part]

        for part in range(2):
            columns = slice(part * 256, (part + 1) * 256)
            even = along_plane(back_high, back_low, 1, 0, columns)
            odd = along_plane(back_high, back_low, 1, 1, columns)
            lower = even + odd
            upper = even - odd
            for side in range(2):
                tile = part * 2 + side
                lanes = slice(side * LANES, (side + 1) * LANES)
                cells[pl.ds(tile, 256, stride=8), :] = lower[:, lanes]
                cells[pl.ds(7 - tile, 256, stride=8), :] = turned(upper[:, lanes])

        for slot in range(2):

            for turn in range(4):
                own, partner, own_offset, partner_offset, active = geometry(
                    solve_index(turn, slot)
                )
                number = turn * 2 + slot
                potential = cells[number * ROWS : (number + 1) * ROWS, :]
                back = [-offset for offset in own_offset]
                term = placed(potential * second[number], back, turn)
                if turn == 0:
                    force[...] = term
                else:
                    force[...] = force[...] + term
            total = force[...]
            field = total.reshape(BOX, 8, LANES)
            peak = jnp.max(
                jnp.max(jnp.abs(field), axis=1, keepdims=True), axis=2, keepdims=True
            )
            safe = jnp.maximum(peak, 1e-30)
            code = jnp.floor(field * (LARGEST / safe) + 0.5)
            coded[:, half * 2 + slot] = code.astype(jnp.int32).astype(jnp.int16)
            step_size = jnp.broadcast_to(safe * (1.0 / LARGEST), (BOX, 1, LANES))
            if slot == 0:
                scales[half * 32 : half * 32 + 32] = step_size
            else:
                lanes = lax.broadcasted_iota(jnp.int32, (BOX, 1, LANES), 2)
                kept = scales[half * 32 : half * 32 + 32]
                scales[half * 32 : half * 32 + 32] = jnp.where(lanes >= slot, step_size, kept)
        send(half)

    drain(planes.at[pl.ds(0, 31)], send_slab)
    drain(boxes.at[pl.ds(0, 7)], send_pair)
    drain(scales_in, from_scales)
    drain(coded_in, from_coded)
    for member in range(4):
        value = (
            coded_in[:, member].astype(jnp.int32).astype(jnp.float32)
            * scales_in[
                (member // 2) * 32 : (member // 2) * 32 + 32, :, member % 2 : member % 2 + 1
            ]
        )
        for team in range(32):
            row = (team * 4 + member) * 8
            stage[row : row + 8, :] = value[team]
    for tile in range(8):
        out_ref[:, tile * LANES : (tile + 1) * LANES] = stage[pl.ds(tile, 128, stride=8), :]
    drain(coded.at[pl.ds(0, 31)], send_coded)
    drain(scales.at[pl.ds(0, 62)], send_scales)


def shards(orbitals, centers, matchings):
    spread_y, spread_z, line, response = tables()
    vmem = pl.BlockSpec(memory_space=pltpu.VMEM)
    one = pltpu.SemaphoreType.DMA
    hbm = pl.BlockSpec(memory_space=pltpu.HBM)
    return pl.pallas_call(
        kernel,
        out_shape=jax.ShapeDtypeStruct((128, 1024), jnp.float32),
        in_specs=[hbm] * 7,
        out_specs=vmem,
        scratch_shapes=[
            pltpu.SMEM((3, 1024), jnp.int32),
            pltpu.SMEM((1, 4, 32), jnp.int32),
            pltpu.VMEM((128, 1024), jnp.bfloat16),
            pltpu.VMEM(spread_y.shape, jnp.float32),
            pltpu.VMEM(spread_z.shape, jnp.float32),
            pltpu.VMEM(line.shape, jnp.bfloat16),
            pltpu.VMEM(response.shape, jnp.float32),
            pltpu.VMEM((1024, LANES), jnp.float32),
            pltpu.VMEM((32, 4, 8, LANES), jnp.bfloat16),
            pltpu.VMEM((8, 32, 4, 8, LANES), jnp.bfloat16),
            pltpu.VMEM((2, 2, 512, 512), jnp.bfloat16),
            pltpu.VMEM((2, 2, 512, 512), jnp.bfloat16),
            pltpu.VMEM((4, ROWS + 2 * MARGIN, LANES), jnp.float32),
            pltpu.VMEM((16, ROWS, LANES), jnp.float32),
            pltpu.VMEM((8, ROWS, LANES), jnp.float32),
            pltpu.VMEM((8 * ROWS, LANES), jnp.float32),
            pltpu.VMEM((2, 256, 512), jnp.bfloat16),
            pltpu.VMEM((2, 256, 512), jnp.bfloat16),
            pltpu.VMEM((2, 256, 512), jnp.bfloat16),
            pltpu.VMEM((2, 256, 512), jnp.bfloat16),
            pltpu.VMEM((256, 2048), jnp.bfloat16),
            pltpu.VMEM((256, 2048), jnp.bfloat16),
            pltpu.VMEM((ROWS, LANES), jnp.float32),
            pltpu.VMEM((32, 4, 8, LANES), jnp.int16),
            pltpu.VMEM((64, 1, LANES), jnp.float32),
            pltpu.VMEM((32, 4, 8, LANES), jnp.int16),
            pltpu.VMEM((64, 1, LANES), jnp.float32),
            one((7,)),
            one,
            one,
            one((8,)),
            one((8,)),
            one((8,)),
            one((8,)),
            one,
            one,
            one,
            one,
            one,
        ],
        compiler_params=pltpu.CompilerParams(
            collective_id=0, has_side_effects=True, vmem_limit_bytes=63 * 1024 * 1024
        ),
    )(centers.T, matchings, orbitals, spread_y, spread_z, line, response)


def solution(mesh):
    in_specs = (P("pair", "slab"), P(), P("slab", None, None))
    out_specs = P("pair", "slab")
    return jax.shard_map(shards, mesh=mesh, in_specs=in_specs, out_specs=out_specs, check_vma=False)
```

```python
import jax
import jax.numpy as jnp
import numpy as np
from jax import lax
from jax.experimental import pallas as pl
from jax.experimental.pallas import tpu as pltpu
from jax.sharding import PartitionSpec as P

BOX = 32
STEPS = 16
CUT2 = 192
SCREEN = 0.1
LOWER_BOUND = 0.1
UPPER_BOUND = 12.1
ROWS = 256
LANES = 128
MARGIN = 72
LARGEST = 32767.0
HOPS = (0, 1, -1, 2, -2, 3, -3, 4)
NEAR_LAG = 4
FAR_LAG = 8
RELAYED = 4
WAYS = 4
MESH = pl.DeviceIdType.MESH


def sine_table():
    index = np.arange(1, BOX + 1)
    return np.sqrt(2.0 / (BOX + 1)) * np.sin(np.pi * np.outer(index, index) / (BOX + 1))


def filter_table():
    line = 2.0 * np.cos(np.pi * np.arange(1, BOX + 1) / (BOX + 1))
    total = line[:, None, None] + line[None, :, None] + line[None, None, :]
    operator = 6.0 + SCREEN - total
    middle = (UPPER_BOUND + LOWER_BOUND) / 2.0
    spread = (UPPER_BOUND - LOWER_BOUND) / 2.0
    ratio = middle / spread
    solution = np.zeros_like(operator)
    residual = np.ones_like(operator)
    direction = residual / middle
    factor = 1.0 / ratio
    for _ in range(STEPS):
        solution = solution + direction
        residual = residual - operator * direction
        factor_next = 1.0 / (2.0 * ratio - factor)
        direction = factor_next * factor * direction + 2.0 * factor_next / spread * residual
        factor = factor_next
    return solution


def tables():
    sine = sine_table()
    high = sine.astype(jnp.bfloat16).astype(np.float64)
    low = sine - high
    line_high = np.kron(np.eye(4), high)
    line_low = np.kron(np.eye(4), low)
    line = np.block([[line_high, line_high], [line_low, line_low]]).astype(jnp.bfloat16)
    order = np.concatenate([np.arange(0, BOX, 2), np.arange(1, BOX, 2)])
    response = filter_table()[:, order, :].reshape(BOX, 4, 1, 256)
    response = np.tile(response, (1, 1, 2, 1)).reshape(BOX, 2048)
    half = BOX // 2
    waves_y = np.stack([sine[:half, order[:half]], sine[:half, order[half:]]])
    spread_waves = np.repeat(waves_y, BOX, axis=2)
    spread_cells = np.repeat(waves_y.transpose(0, 2, 1), BOX, axis=2)
    spread_y = np.stack([spread_waves, spread_cells])
    spread_z = np.tile(sine, (1, half))
    return (
        spread_y.astype(np.float32),
        spread_z.astype(np.float32),
        line,
        response.astype(np.float32),
    )


def split(value):
    high = value.astype(jnp.bfloat16)
    low = (value - high.astype(jnp.float32)).astype(jnp.bfloat16)
    return high, low


def dot(left, right):
    return jnp.dot(left, right, preferred_element_type=jnp.float32)


def drain(ref, semaphore):
    pltpu.make_async_copy(ref, ref, semaphore).wait()


def kernel(
    centers_table,
    match_table,
    orbitals_table,
    spread_y_table,
    spread_z_table,
    line_table,
    response_table,
    out_ref,
    centers_ref,
    match_ref,
    orbitals_ref,
    spread_y_ref,
    spread_z_ref,
    line_ref,
    response_ref,
    stage,
    planes,
    boxes,
    plane_high,
    plane_low,
    padded,
    first,
    second,
    cells,
    left_high,
    left_low,
    back_high,
    back_low,
    lines,
    lines_back,
    force,
    coded,
    scales,
    coded_in,
    scales_in,
    tables_done,
    send_slab,
    send_pair,
    from_slab,
    from_left,
    from_right,
    from_far,
    from_mate,
    send_coded,
    send_scales,
    from_coded,
    from_scales,
):
    slab = lax.axis_index("slab")
    pair = lax.axis_index("pair")
    z = slab // 4
    y = slab % 4
    x = pair // 2
    core = pair % 2
    right = ((x + 1) % 4) * 2 + core
    left = ((x + 3) % 4) * 2 + core
    far = ((x + 2) % 4) * 2 + core
    mate = x * 2 + 1 - core

    barrier = pltpu.get_barrier_semaphore()

    @pl.loop(1, 32)
    def _(step):
        pl.semaphore_signal(
            barrier, inc=1, device_id=((slab + step) % 32, pair), device_id_type=MESH
        )

    for other in (right, left, mate, far):
        pl.semaphore_signal(barrier, inc=1, device_id=(slab, other), device_id_type=MESH)

    copies = [
        pltpu.make_async_copy(table, ref, tables_done.at[index])
        for index, (table, ref) in enumerate(
            [
                (orbitals_table, orbitals_ref),
                (centers_table, centers_ref),
                (match_table, match_ref),
                (spread_y_table, spread_y_ref),
                (spread_z_table, spread_z_ref),
                (line_table, line_ref),
                (response_table, response_ref),
            ]
        )
    ]
    for copy in copies:
        copy.start()

    copies[0].wait()
    for tile in range(8):
        stage[pl.ds(tile, 128, stride=8), :] = orbitals_ref[
            :, tile * LANES : (tile + 1) * LANES
        ].astype(jnp.float32)
    planes[...] = stage[...].reshape(32, 4, 8, LANES).astype(jnp.bfloat16)
    padded[...] = jnp.zeros_like(padded)
    lane = lax.broadcasted_iota(jnp.int32, (8, LANES), 1)
    line = 4 * lax.broadcasted_iota(jnp.int32, (8, LANES), 0) + (lane >> 5)
    point = lane & 31

    for copy in copies[1:]:
        copy.wait()
    for way in range(2):
        for parity in range(2):

            @pl.loop(0, 16)
            def _(row):
                product = spread_y_ref[way, parity, pl.ds(row, 1), :] * spread_z_ref[...]
                high, low = split(product)
                rows = pl.ds(pl.multiple_of(row * 32, 32), 32)
                plane_high[way, parity, rows, :] = high
                plane_low[way, parity, rows, :] = low

    pl.semaphore_wait(barrier, 35)

    for index, hop in enumerate(HOPS):
        target_z = (z + hop + 8) % 8
        for turn in range(4):
            if hop == 0 and turn == 0:
                pltpu.make_async_copy(
                    planes.at[slab], boxes.at[pair, slab], from_slab.at[0]
                ).start()
                continue
            target = target_z * 4 + (y + turn) % 4
            pltpu.make_async_remote_copy(
                src_ref=planes.at[target],
                dst_ref=boxes.at[pair, slab],
                send_sem=send_slab,
                recv_sem=from_slab.at[index],
                device_id=(target, pair),
                device_id_type=MESH,
            ).start()

    def chunk(owner, index):
        return boxes.at[owner, pl.ds(((z - HOPS[index] + 8) % 8) * 4, 4)]

    def transfer(owner, index, arrival, target):
        return pltpu.make_async_remote_copy(
            src_ref=chunk(owner, index),
            dst_ref=chunk(owner, index),
            send_sem=send_pair,
            recv_sem=arrival,
            device_id=(slab, target),
            device_id_type=MESH,
        )

    def center(member, axis):
        return centers_ref[axis, ((member >> 2) * 32 + slab) * 4 + (member & 3)]

    def box(member):
        return boxes[member >> 2, :, member & 3].astype(jnp.float32).reshape(ROWS, LANES)

    def placed(field, offset, way):
        flat = offset[0] * 1024 + offset[1] * 32 + offset[2]
        turn = flat & 127
        rows = flat >> 7
        padded[way, MARGIN : MARGIN + ROWS, :] = pltpu.roll(field, turn, axis=1)
        near = padded[way, pl.ds(MARGIN - rows, ROWS), :]
        far = padded[way, pl.ds(MARGIN - 1 - rows, ROWS), :]
        from_line = line - offset[1]
        from_point = point - offset[2]
        inside = (
            (from_line >= 0) & (from_line < BOX) & (from_point >= 0) & (from_point < BOX)
        )
        keep_near = inside & (lane >= turn)
        keep_far = inside & (lane < turn)
        near = near.reshape(BOX, 8, LANES)
        far = far.reshape(BOX, 8, LANES)
        zero = jnp.zeros_like(near)
        picked = jnp.where(keep_near[None], near, jnp.where(keep_far[None], far, zero))
        return picked.reshape(ROWS, LANES)

    def geometry(index):
        own = pair * 4 + (index & 3)
        partner = match_ref[0, index >> 2, own]
        own_center = [center(own, axis) for axis in range(3)]
        partner_center = [center(partner, axis) for axis in range(3)]
        anchor = [(x + y) >> 1 for x, y in zip(own_center, partner_center)]
        own_offset = [x - g for x, g in zip(own_center, anchor)]
        partner_offset = [y - g for y, g in zip(partner_center, anchor)]
        distance = sum((x - y) * (x - y) for x, y in zip(own_center, partner_center))
        active = jnp.where(distance <= CUT2, 1.0, 0.0).astype(jnp.float32)
        return own, partner, own_offset, partner_offset, active

    for step in range(8 + FAR_LAG):
        if step < 8:
            transfer(pair, step, from_slab.at[step], mate).wait_recv()
            transfer(pair, step, from_left.at[step], right).start()
            transfer(pair, step, from_right.at[step], left).start()
            if step >= RELAYED:
                transfer(pair, step, from_far.at[step], far).start()
            transfer(pair, step, from_mate, mate).start()
        else:

            @pl.loop(2 * (step - 8), 2 * (step - 7))
            def _(index):
                own, partner, own_offset, partner_offset, active = geometry(index)
                first[index] = active * placed(box(own), own_offset, 0)

        index = step - NEAR_LAG
        if 0 <= index < 8:
            transfer(left, index, from_left.at[index], mate).wait_recv()
            if index < RELAYED and index % 2 == 0:
                transfer(left, index, from_far.at[index], right).start()
            transfer(left, index, from_mate, mate).start()
            transfer(right, index, from_right.at[index], mate).wait_recv()
            if index < RELAYED and index % 2 == 1:
                transfer(right, index, from_far.at[index], left).start()
            transfer(right, index, from_mate, mate).start()
        index = step - FAR_LAG
        if 0 <= index < 8:
            transfer(far, index, from_far.at[index], mate).wait_recv()
            transfer(far, index, from_mate, mate).start()

    drain(boxes.at[pl.ds(0, 4)], from_mate)

    def turned(block):
        swapped = pltpu.roll(block, 64, axis=1)
        odd = (lax.broadcasted_iota(jnp.int32, block.shape, 1) & 32) != 0
        return jnp.where(odd, pltpu.roll(swapped, 32, axis=1), pltpu.roll(swapped, 96, axis=1))

    def along_plane(high_ref, low_ref, way, parity, columns):
        high_table = plane_high[way, parity, :, columns]
        total = dot(high_ref[parity], high_table)
        total = total + dot(low_ref[parity], high_table)
        return total + dot(high_ref[parity], plane_low[way, parity, :, columns])

    def send(half):
        slots = pl.ds(half * 2, 2)
        pltpu.make_async_copy(
            coded.at[slab, slots], coded_in.at[slab, slots], from_coded
        ).start()
        pltpu.make_async_copy(
            scales.at[half * 32 + slab], scales_in.at[half * 32 + slab], from_scales
        ).start()

        for hop in reversed(HOPS):
            for turn in (2, 1, 3, 0):
                if hop == 0 and turn == 0:
                    continue
                target = (z + hop + 8) % 8 * 4 + (y + turn) % 4
                pltpu.make_async_remote_copy(
                    src_ref=coded.at[target, slots],
                    dst_ref=coded_in.at[slab, slots],
                    send_sem=send_coded,
                    recv_sem=from_coded,
                    device_id=(target, pair),
                    device_id_type=MESH,
                ).start()
                pltpu.make_async_remote_copy(
                    src_ref=scales.at[half * 32 + target],
                    dst_ref=scales_in.at[half * 32 + slab],
                    send_sem=send_scales,
                    recv_sem=from_scales,
                    device_id=(target, pair),
                    device_id_type=MESH,
                ).start()

    for half in range(2):

        def solve_index(turn, slot):
            return turn * 4 + half * 2 + slot

        @pl.loop(0, 8 // WAYS)
        def _(step):
            for way in range(WAYS):
                number = step * WAYS + way
                index = solve_index(number >> 1, number & 1)
                own, partner, own_offset, partner_offset, active = geometry(index)
                second_field = placed(box(partner), partner_offset, way)
                second[number] = second_field
                cells[pl.ds(pl.multiple_of(number * ROWS, ROWS), ROWS), :] = (
                    first[index] * second_field
                )

        for tile in range(4):
            lower = cells[pl.ds(tile, 256, stride=8), :]
            upper = turned(cells[pl.ds(7 - tile, 256, stride=8), :])
            columns = slice(tile * LANES, (tile + 1) * LANES)
            for parity, value in enumerate((lower + upper, lower - upper)):
                high, low = split(value)
                left_high[parity, :, columns] = high
                left_low[parity, :, columns] = low

        for tile in range(4):
            parity = tile // 2
            columns = slice((tile % 2) * 256, (tile % 2 + 1) * 256)
            high, low = split(along_plane(left_high, left_low, 0, parity, columns))
            for group in range(2):
                rows = slice(group * 128, (group + 1) * 128)
                part = slice((tile * 2 + group) * 256, (tile * 2 + group + 1) * 256)
                lines[:128, part] = high[rows]
                lines[128:, part] = low[rows]

        for start in range(0, 2048, 512):
            columns = slice(start, start + 512)
            both = dot(line_ref[...], lines[:, columns])
            response = jnp.tile(response_ref[:, columns], (4, 1))
            high, low = split((both[:128] + both[128:]) * response)
            lines_back[:128, columns] = high
            lines_back[128:, columns] = low

        for start in range(0, 2048, 512):
            columns = slice(start, start + 512)
            both = dot(line_ref[...], lines_back[:, columns])
            high, low = split(both[:128] + both[128:])
            for block in range(2):
                place = start // 256 + block
                tile = place // 2
                group = place % 2
                rows = slice(group * 128, (group + 1) * 128)
                part = slice(block * 256, (block + 1) * 256)
                columns = slice((tile % 2) * 256, (tile % 2 + 1) * 256)
                back_high[tile // 2, rows, columns] = high[:, part]
                back_low[tile // 2, rows, columns] = low[:, part]

        for part in range(2):
            columns = slice(part * 256, (part + 1) * 256)
            even = along_plane(back_high, back_low, 1, 0, columns)
            odd = along_plane(back_high, back_low, 1, 1, columns)
            lower = even + odd
            upper = even - odd
            for side in range(2):
                tile = part * 2 + side
                lanes = slice(side * LANES, (side + 1) * LANES)
                cells[pl.ds(tile, 256, stride=8), :] = lower[:, lanes]
                cells[pl.ds(7 - tile, 256, stride=8), :] = turned(upper[:, lanes])

        for slot in range(2):

            for turn in range(4):
                own, partner, own_offset, partner_offset, active = geometry(
                    solve_index(turn, slot)
                )
                number = turn * 2 + slot
                potential = cells[number * ROWS : (number + 1) * ROWS, :]
                back = [-offset for offset in own_offset]
                term = placed(potential * second[number], back, turn)
                if turn == 0:
                    force[...] = term
                else:
                    force[...] = force[...] + term
            total = force[...]
            field = total.reshape(BOX, 8, LANES)
            peak = jnp.max(
                jnp.max(jnp.abs(field), axis=1, keepdims=True), axis=2, keepdims=True
            )
            safe = jnp.maximum(peak, 1e-30)
            code = jnp.floor(field * (LARGEST / safe) + 0.5)
            coded[:, half * 2 + slot] = code.astype(jnp.int32).astype(jnp.int16)
            step_size = jnp.broadcast_to(safe * (1.0 / LARGEST), (BOX, 1, LANES))
            if slot == 0:
                scales[half * 32 : half * 32 + 32] = step_size
            else:
                lanes = lax.broadcasted_iota(jnp.int32, (BOX, 1, LANES), 2)
                kept = scales[half * 32 : half * 32 + 32]
                scales[half * 32 : half * 32 + 32] = jnp.where(lanes >= slot, step_size, kept)
        send(half)

    drain(planes.at[pl.ds(0, 31)], send_slab)
    drain(boxes.at[pl.ds(0, 7)], send_pair)
    drain(scales_in, from_scales)
    drain(coded_in, from_coded)
    for member in range(4):
        value = (
            coded_in[:, member].astype(jnp.int32).astype(jnp.float32)
            * scales_in[
                (member // 2) * 32 : (member // 2) * 32 + 32, :, member % 2 : member % 2 + 1
            ]
        )
        for team in range(32):
            row = (team * 4 + member) * 8
            stage[row : row + 8, :] = value[team]
    for tile in range(8):
        out_ref[:, tile * LANES : (tile + 1) * LANES] = stage[pl.ds(tile, 128, stride=8), :]
    drain(coded.at[pl.ds(0, 31)], send_coded)
    drain(scales.at[pl.ds(0, 62)], send_scales)


def shards(orbitals, centers, matchings):
    spread_y, spread_z, line, response = tables()
    vmem = pl.BlockSpec(memory_space=pltpu.VMEM)
    one = pltpu.SemaphoreType.DMA
    hbm = pl.BlockSpec(memory_space=pltpu.HBM)
    return pl.pallas_call(
        kernel,
        out_shape=jax.ShapeDtypeStruct((128, 1024), jnp.float32),
        in_specs=[hbm] * 7,
        out_specs=vmem,
        scratch_shapes=[
            pltpu.SMEM((3, 1024), jnp.int32),
            pltpu.SMEM((1, 4, 32), jnp.int32),
            pltpu.VMEM((128, 1024), jnp.bfloat16),
            pltpu.VMEM(spread_y.shape, jnp.float32),
            pltpu.VMEM(spread_z.shape, jnp.float32),
            pltpu.VMEM(line.shape, jnp.bfloat16),
            pltpu.VMEM(response.shape, jnp.float32),
            pltpu.VMEM((1024, LANES), jnp.float32),
            pltpu.VMEM((32, 4, 8, LANES), jnp.bfloat16),
            pltpu.VMEM((8, 32, 4, 8, LANES), jnp.bfloat16),
            pltpu.VMEM((2, 2, 512, 512), jnp.bfloat16),
            pltpu.VMEM((2, 2, 512, 512), jnp.bfloat16),
            pltpu.VMEM((4, ROWS + 2 * MARGIN, LANES), jnp.float32),
            pltpu.VMEM((16, ROWS, LANES), jnp.float32),
            pltpu.VMEM((8, ROWS, LANES), jnp.float32),
            pltpu.VMEM((8 * ROWS, LANES), jnp.float32),
            pltpu.VMEM((2, 256, 512), jnp.bfloat16),
            pltpu.VMEM((2, 256, 512), jnp.bfloat16),
            pltpu.VMEM((2, 256, 512), jnp.bfloat16),
            pltpu.VMEM((2, 256, 512), jnp.bfloat16),
            pltpu.VMEM((256, 2048), jnp.bfloat16),
            pltpu.VMEM((256, 2048), jnp.bfloat16),
            pltpu.VMEM((ROWS, LANES), jnp.float32),
            pltpu.VMEM((32, 4, 8, LANES), jnp.int16),
            pltpu.VMEM((64, 1, LANES), jnp.float32),
            pltpu.VMEM((32, 4, 8, LANES), jnp.int16),
            pltpu.VMEM((64, 1, LANES), jnp.float32),
            one((7,)),
            one,
            one,
            one((8,)),
            one((8,)),
            one((8,)),
            one((8,)),
            one,
            one,
            one,
            one,
            one,
        ],
        compiler_params=pltpu.CompilerParams(
            collective_id=0, has_side_effects=True, vmem_limit_bytes=63 * 1024 * 1024
        ),
    )(centers.T, matchings, orbitals, spread_y, spread_z, line, response)


def solution(mesh):
    in_specs = (P("pair", "slab"), P(), P("slab", None, None))
    out_specs = P("pair", "slab")
    return jax.shard_map(shards, mesh=mesh, in_specs=in_specs, out_specs=out_specs, check_vma=False)
```

```python
import jax
import jax.numpy as jnp
import numpy as np
from jax import lax
from jax.experimental import pallas as pl
from jax.experimental.pallas import tpu as pltpu
from jax.sharding import PartitionSpec as P

BOX = 32
STEPS = 16
CUT2 = 192
SCREEN = 0.1
LOWER_BOUND = 0.1
UPPER_BOUND = 12.1
ROWS = 256
LANES = 128
MARGIN = 72
LARGEST = 32767.0
HOPS = (0, 1, -1, 2, -2, 3, -3, 4)
NEAR_LAG = 4
FAR_LAG = 8
RELAYED = 4
WAYS = 4
MESH = pl.DeviceIdType.MESH


def sine_table():
    index = np.arange(1, BOX + 1)
    return np.sqrt(2.0 / (BOX + 1)) * np.sin(np.pi * np.outer(index, index) / (BOX + 1))


def filter_table():
    line = 2.0 * np.cos(np.pi * np.arange(1, BOX + 1) / (BOX + 1))
    total = line[:, None, None] + line[None, :, None] + line[None, None, :]
    operator = 6.0 + SCREEN - total
    middle = (UPPER_BOUND + LOWER_BOUND) / 2.0
    spread = (UPPER_BOUND - LOWER_BOUND) / 2.0
    ratio = middle / spread
    solution = np.zeros_like(operator)
    residual = np.ones_like(operator)
    direction = residual / middle
    factor = 1.0 / ratio
    for _ in range(STEPS):
        solution = solution + direction
        residual = residual - operator * direction
        factor_next = 1.0 / (2.0 * ratio - factor)
        direction = factor_next * factor * direction + 2.0 * factor_next / spread * residual
        factor = factor_next
    return solution


def tables():
    sine = sine_table()
    high = sine.astype(jnp.bfloat16).astype(np.float64)
    low = sine - high
    line_high = np.kron(np.eye(4), high)
    line_low = np.kron(np.eye(4), low)
    line = np.block([[line_high, line_high], [line_low, line_low]]).astype(jnp.bfloat16)
    order = np.concatenate([np.arange(0, BOX, 2), np.arange(1, BOX, 2)])
    response = filter_table()[:, order, :].reshape(BOX, 4, 1, 256)
    response = np.tile(response, (1, 1, 2, 1)).reshape(BOX, 2048)
    half = BOX // 2
    waves_y = np.stack([sine[:half, order[:half]], sine[:half, order[half:]]])
    spread_waves = np.repeat(waves_y, BOX, axis=2)
    spread_cells = np.repeat(waves_y.transpose(0, 2, 1), BOX, axis=2)
    spread_y = np.stack([spread_waves, spread_cells])
    spread_z = np.tile(sine, (1, half))
    return (
        spread_y.astype(np.float32),
        spread_z.astype(np.float32),
        line,
        response.astype(np.float32),
    )


def split(value):
    high = value.astype(jnp.bfloat16)
    low = (value - high.astype(jnp.float32)).astype(jnp.bfloat16)
    return high, low


def dot(left, right):
    return jnp.dot(left, right, preferred_element_type=jnp.float32)


def drain(ref, semaphore):
    pltpu.make_async_copy(ref, ref, semaphore).wait()


def kernel(
    centers_table,
    match_table,
    orbitals_table,
    spread_y_table,
    spread_z_table,
    line_table,
    response_table,
    out_ref,
    centers_ref,
    match_ref,
    orbitals_ref,
    spread_y_ref,
    spread_z_ref,
    line_ref,
    response_ref,
    stage,
    planes,
    boxes,
    plane_high,
    plane_low,
    padded,
    first,
    second,
    cells,
    left_high,
    left_low,
    back_high,
    back_low,
    lines,
    lines_back,
    force,
    coded,
    scales,
    coded_in,
    scales_in,
    tables_done,
    send_slab,
    send_pair,
    from_slab,
    from_left,
    from_right,
    from_far,
    from_mate,
    send_coded,
    send_scales,
    from_coded,
    from_scales,
):
    slab = lax.axis_index("slab")
    pair = lax.axis_index("pair")
    z = slab // 4
    y = slab % 4
    x = pair // 2
    core = pair % 2
    right = ((x + 1) % 4) * 2 + core
    left = ((x + 3) % 4) * 2 + core
    far = ((x + 2) % 4) * 2 + core
    mate = x * 2 + 1 - core

    barrier = pltpu.get_barrier_semaphore()

    @pl.loop(1, 32)
    def _(step):
        pl.semaphore_signal(
            barrier, inc=1, device_id=((slab + step) % 32, pair), device_id_type=MESH
        )

    for other in (right, left, mate, far):
        pl.semaphore_signal(barrier, inc=1, device_id=(slab, other), device_id_type=MESH)

    copies = [
        pltpu.make_async_copy(table, ref, tables_done.at[index])
        for index, (table, ref) in enumerate(
            [
                (orbitals_table, orbitals_ref),
                (centers_table, centers_ref),
                (match_table, match_ref),
                (spread_y_table, spread_y_ref),
                (spread_z_table, spread_z_ref),
                (line_table, line_ref),
                (response_table, response_ref),
            ]
        )
    ]
    for copy in copies:
        copy.start()

    copies[0].wait()
    for tile in range(8):
        stage[pl.ds(tile, 128, stride=8), :] = orbitals_ref[
            :, tile * LANES : (tile + 1) * LANES
        ].astype(jnp.float32)
    planes[...] = stage[...].reshape(32, 4, 8, LANES).astype(jnp.bfloat16)
    padded[...] = jnp.zeros_like(padded)
    lane = lax.broadcasted_iota(jnp.int32, (8, LANES), 1)
    line = 4 * lax.broadcasted_iota(jnp.int32, (8, LANES), 0) + (lane >> 5)
    point = lane & 31

    for copy in copies[1:]:
        copy.wait()
    for way in range(2):
        for parity in range(2):

            @pl.loop(0, 16)
            def _(row):
                product = spread_y_ref[way, parity, pl.ds(row, 1), :] * spread_z_ref[...]
                high, low = split(product)
                rows = pl.ds(pl.multiple_of(row * 32, 32), 32)
                plane_high[way, parity, rows, :] = high
                plane_low[way, parity, rows, :] = low

    pl.semaphore_wait(barrier, 35)

    for index, hop in enumerate(HOPS):
        target_z = (z + hop + 8) % 8
        for turn in (2, 1, 3, 0):
            if hop == 0 and turn == 0:
                pltpu.make_async_copy(
                    planes.at[slab], boxes.at[pair, slab], from_slab.at[0]
                ).start()
                continue
            target = target_z * 4 + (y + turn) % 4
            pltpu.make_async_remote_copy(
                src_ref=planes.at[target],
                dst_ref=boxes.at[pair, slab],
                send_sem=send_slab,
                recv_sem=from_slab.at[index],
                device_id=(target, pair),
                device_id_type=MESH,
            ).start()

    def chunk(owner, index):
        return boxes.at[owner, pl.ds(((z - HOPS[index] + 8) % 8) * 4, 4)]

    def transfer(owner, index, arrival, target):
        return pltpu.make_async_remote_copy(
            src_ref=chunk(owner, index),
            dst_ref=chunk(owner, index),
            send_sem=send_pair,
            recv_sem=arrival,
            device_id=(slab, target),
            device_id_type=MESH,
        )

    def center(member, axis):
        return centers_ref[axis, ((member >> 2) * 32 + slab) * 4 + (member & 3)]

    def box(member):
        return boxes[member >> 2, :, member & 3].astype(jnp.float32).reshape(ROWS, LANES)

    def placed(field, offset, way):
        flat = offset[0] * 1024 + offset[1] * 32 + offset[2]
        turn = flat & 127
        rows = flat >> 7
        padded[way, MARGIN : MARGIN + ROWS, :] = pltpu.roll(field, turn, axis=1)
        near = padded[way, pl.ds(MARGIN - rows, ROWS), :]
        far = padded[way, pl.ds(MARGIN - 1 - rows, ROWS), :]
        from_line = line - offset[1]
        from_point = point - offset[2]
        inside = (
            (from_line >= 0) & (from_line < BOX) & (from_point >= 0) & (from_point < BOX)
        )
        keep_near = inside & (lane >= turn)
        keep_far = inside & (lane < turn)
        near = near.reshape(BOX, 8, LANES)
        far = far.reshape(BOX, 8, LANES)
        zero = jnp.zeros_like(near)
        picked = jnp.where(keep_near[None], near, jnp.where(keep_far[None], far, zero))
        return picked.reshape(ROWS, LANES)

    def geometry(index):
        own = pair * 4 + (index & 3)
        partner = match_ref[0, index >> 2, own]
        own_center = [center(own, axis) for axis in range(3)]
        partner_center = [center(partner, axis) for axis in range(3)]
        anchor = [(x + y) >> 1 for x, y in zip(own_center, partner_center)]
        own_offset = [x - g for x, g in zip(own_center, anchor)]
        partner_offset = [y - g for y, g in zip(partner_center, anchor)]
        distance = sum((x - y) * (x - y) for x, y in zip(own_center, partner_center))
        active = jnp.where(distance <= CUT2, 1.0, 0.0).astype(jnp.float32)
        return own, partner, own_offset, partner_offset, active

    for step in range(8 + FAR_LAG):
        if step < 8:
            transfer(pair, step, from_slab.at[step], mate).wait_recv()
            transfer(pair, step, from_left.at[step], right).start()
            transfer(pair, step, from_right.at[step], left).start()
            if step >= RELAYED:
                transfer(pair, step, from_far.at[step], far).start()
            transfer(pair, step, from_mate, mate).start()
        else:

            @pl.loop(2 * (step - 8), 2 * (step - 7))
            def _(index):
                own, partner, own_offset, partner_offset, active = geometry(index)
                first[index] = active * placed(box(own), own_offset, 0)

        index = step - NEAR_LAG
        if 0 <= index < 8:
            transfer(left, index, from_left.at[index], mate).wait_recv()
            if index < RELAYED and index % 2 == 0:
                transfer(left, index, from_far.at[index], right).start()
            transfer(left, index, from_mate, mate).start()
            transfer(right, index, from_right.at[index], mate).wait_recv()
            if index < RELAYED and index % 2 == 1:
                transfer(right, index, from_far.at[index], left).start()
            transfer(right, index, from_mate, mate).start()
        index = step - FAR_LAG
        if 0 <= index < 8:
            transfer(far, index, from_far.at[index], mate).wait_recv()
            transfer(far, index, from_mate, mate).start()

    drain(boxes.at[pl.ds(0, 4)], from_mate)

    def turned(block):
        swapped = pltpu.roll(block, 64, axis=1)
        odd = (lax.broadcasted_iota(jnp.int32, block.shape, 1) & 32) != 0
        return jnp.where(odd, pltpu.roll(swapped, 32, axis=1), pltpu.roll(swapped, 96, axis=1))

    def along_plane(high_ref, low_ref, way, parity, columns):
        high_table = plane_high[way, parity, :, columns]
        total = dot(high_ref[parity], high_table)
        total = total + dot(low_ref[parity], high_table)
        return total + dot(high_ref[parity], plane_low[way, parity, :, columns])

    def send(half):
        slots = pl.ds(half * 2, 2)
        pltpu.make_async_copy(
            coded.at[slab, slots], coded_in.at[slab, slots], from_coded.at[half]
        ).start()
        pltpu.make_async_copy(
            scales.at[half * 32 + slab], scales_in.at[half * 32 + slab], from_scales.at[half]
        ).start()

        for hop in reversed(HOPS):
            for turn in (2, 1, 3, 0):
                if hop == 0 and turn == 0:
                    continue
                target = (z + hop + 8) % 8 * 4 + (y + turn) % 4
                pltpu.make_async_remote_copy(
                    src_ref=coded.at[target, slots],
                    dst_ref=coded_in.at[slab, slots],
                    send_sem=send_coded,
                    recv_sem=from_coded.at[half],
                    device_id=(target, pair),
                    device_id_type=MESH,
                ).start()
                pltpu.make_async_remote_copy(
                    src_ref=scales.at[half * 32 + target],
                    dst_ref=scales_in.at[half * 32 + slab],
                    send_sem=send_scales,
                    recv_sem=from_scales.at[half],
                    device_id=(target, pair),
                    device_id_type=MESH,
                ).start()

    for half in range(2):

        def solve_index(turn, slot):
            return turn * 4 + half * 2 + slot

        @pl.loop(0, 8 // WAYS)
        def _(step):
            for way in range(WAYS):
                number = step * WAYS + way
                index = solve_index(number >> 1, number & 1)
                own, partner, own_offset, partner_offset, active = geometry(index)
                second_field = placed(box(partner), partner_offset, way)
                second[number] = second_field
                cells[pl.ds(pl.multiple_of(number * ROWS, ROWS), ROWS), :] = (
                    first[index] * second_field
                )

        for tile in range(4):
            lower = cells[pl.ds(tile, 256, stride=8), :]
            upper = turned(cells[pl.ds(7 - tile, 256, stride=8), :])
            columns = slice(tile * LANES, (tile + 1) * LANES)
            for parity, value in enumerate((lower + upper, lower - upper)):
                high, low = split(value)
                left_high[parity, :, columns] = high
                left_low[parity, :, columns] = low

        for tile in range(4):
            parity = tile // 2
            columns = slice((tile % 2) * 256, (tile % 2 + 1) * 256)
            high, low = split(along_plane(left_high, left_low, 0, parity, columns))
            for group in range(2):
                rows = slice(group * 128, (group + 1) * 128)
                part = slice((tile * 2 + group) * 256, (tile * 2 + group + 1) * 256)
                lines[:128, part] = high[rows]
                lines[128:, part] = low[rows]

        for start in range(0, 2048, 512):
            columns = slice(start, start + 512)
            both = dot(line_ref[...], lines[:, columns])
            response = jnp.tile(response_ref[:, columns], (4, 1))
            high, low = split((both[:128] + both[128:]) * response)
            lines_back[:128, columns] = high
            lines_back[128:, columns] = low

        for start in range(0, 2048, 512):
            columns = slice(start, start + 512)
            both = dot(line_ref[...], lines_back[:, columns])
            high, low = split(both[:128] + both[128:])
            for block in range(2):
                place = start // 256 + block
                tile = place // 2
                group = place % 2
                rows = slice(group * 128, (group + 1) * 128)
                part = slice(block * 256, (block + 1) * 256)
                columns = slice((tile % 2) * 256, (tile % 2 + 1) * 256)
                back_high[tile // 2, rows, columns] = high[:, part]
                back_low[tile // 2, rows, columns] = low[:, part]

        for part in range(2):
            columns = slice(part * 256, (part + 1) * 256)
            even = along_plane(back_high, back_low, 1, 0, columns)
            odd = along_plane(back_high, back_low, 1, 1, columns)
            lower = even + odd
            upper = even - odd
            for side in range(2):
                tile = part * 2 + side
                lanes = slice(side * LANES, (side + 1) * LANES)
                cells[pl.ds(tile, 256, stride=8), :] = lower[:, lanes]
                cells[pl.ds(7 - tile, 256, stride=8), :] = turned(upper[:, lanes])

        for slot in range(2):

            for turn in range(4):
                own, partner, own_offset, partner_offset, active = geometry(
                    solve_index(turn, slot)
                )
                number = turn * 2 + slot
                potential = cells[number * ROWS : (number + 1) * ROWS, :]
                back = [-offset for offset in own_offset]
                term = placed(potential * second[number], back, turn)
                if turn == 0:
                    force[...] = term
                else:
                    force[...] = force[...] + term
            total = force[...]
            field = total.reshape(BOX, 8, LANES)
            peak = jnp.max(
                jnp.max(jnp.abs(field), axis=1, keepdims=True), axis=2, keepdims=True
            )
            safe = jnp.maximum(peak, 1e-30)
            code = jnp.floor(field * (LARGEST / safe) + 0.5)
            coded[:, half * 2 + slot] = code.astype(jnp.int32).astype(jnp.int16)
            step_size = jnp.broadcast_to(safe * (1.0 / LARGEST), (BOX, 1, LANES))
            if slot == 0:
                scales[half * 32 : half * 32 + 32] = step_size
            else:
                lanes = lax.broadcasted_iota(jnp.int32, (BOX, 1, LANES), 2)
                kept = scales[half * 32 : half * 32 + 32]
                scales[half * 32 : half * 32 + 32] = jnp.where(lanes >= slot, step_size, kept)
        send(half)

    drain(planes.at[pl.ds(0, 31)], send_slab)
    drain(boxes.at[pl.ds(0, 7)], send_pair)
    for member in range(4):
        if member % 2 == 0:
            half = member // 2
            drain(scales_in.at[pl.ds(half * 32, 32)], from_scales.at[half])
            drain(coded_in.at[:, pl.ds(half * 2, 2)], from_coded.at[half])
        value = (
            coded_in[:, member].astype(jnp.int32).astype(jnp.float32)
            * scales_in[
                (member // 2) * 32 : (member // 2) * 32 + 32, :, member % 2 : member % 2 + 1
            ]
        )
        for team in range(32):
            row = (team * 4 + member) * 8
            stage[row : row + 8, :] = value[team]
    for tile in range(8):
        out_ref[:, tile * LANES : (tile + 1) * LANES] = stage[pl.ds(tile, 128, stride=8), :]
    drain(coded.at[pl.ds(0, 31)], send_coded)
    drain(scales.at[pl.ds(0, 62)], send_scales)


def shards(orbitals, centers, matchings):
    spread_y, spread_z, line, response = tables()
    vmem = pl.BlockSpec(memory_space=pltpu.VMEM)
    one = pltpu.SemaphoreType.DMA
    hbm = pl.BlockSpec(memory_space=pltpu.HBM)
    return pl.pallas_call(
        kernel,
        out_shape=jax.ShapeDtypeStruct((128, 1024), jnp.float32),
        in_specs=[hbm] * 7,
        out_specs=vmem,
        scratch_shapes=[
            pltpu.SMEM((3, 1024), jnp.int32),
            pltpu.SMEM((1, 4, 32), jnp.int32),
            pltpu.VMEM((128, 1024), jnp.bfloat16),
            pltpu.VMEM(spread_y.shape, jnp.float32),
            pltpu.VMEM(spread_z.shape, jnp.float32),
            pltpu.VMEM(line.shape, jnp.bfloat16),
            pltpu.VMEM(response.shape, jnp.float32),
            pltpu.VMEM((1024, LANES), jnp.float32),
            pltpu.VMEM((32, 4, 8, LANES), jnp.bfloat16),
            pltpu.VMEM((8, 32, 4, 8, LANES), jnp.bfloat16),
            pltpu.VMEM((2, 2, 512, 512), jnp.bfloat16),
            pltpu.VMEM((2, 2, 512, 512), jnp.bfloat16),
            pltpu.VMEM((4, ROWS + 2 * MARGIN, LANES), jnp.float32),
            pltpu.VMEM((16, ROWS, LANES), jnp.float32),
            pltpu.VMEM((8, ROWS, LANES), jnp.float32),
            pltpu.VMEM((8 * ROWS, LANES), jnp.float32),
            pltpu.VMEM((2, 256, 512), jnp.bfloat16),
            pltpu.VMEM((2, 256, 512), jnp.bfloat16),
            pltpu.VMEM((2, 256, 512), jnp.bfloat16),
            pltpu.VMEM((2, 256, 512), jnp.bfloat16),
            pltpu.VMEM((256, 2048), jnp.bfloat16),
            pltpu.VMEM((256, 2048), jnp.bfloat16),
            pltpu.VMEM((ROWS, LANES), jnp.float32),
            pltpu.VMEM((32, 4, 8, LANES), jnp.int16),
            pltpu.VMEM((64, 1, LANES), jnp.float32),
            pltpu.VMEM((32, 4, 8, LANES), jnp.int16),
            pltpu.VMEM((64, 1, LANES), jnp.float32),
            one((7,)),
            one,
            one,
            one((8,)),
            one((8,)),
            one((8,)),
            one((8,)),
            one,
            one,
            one,
            one((2,)),
            one((2,)),
        ],
        compiler_params=pltpu.CompilerParams(
            collective_id=0, has_side_effects=True, vmem_limit_bytes=63 * 1024 * 1024
        ),
    )(centers.T, matchings, orbitals, spread_y, spread_z, line, response)


def solution(mesh):
    in_specs = (P("pair", "slab"), P(), P("slab", None, None))
    out_specs = P("pair", "slab")
    return jax.shard_map(shards, mesh=mesh, in_specs=in_specs, out_specs=out_specs, check_vma=False)
```
